32 devices in a mesh: ctx: 8 (over z, x), head: 4 (over y, core).
Axes of the slice: x: 2, y: 2, z: 4, core: 2. Of those that a mesh axis runs over, the one named last changes fastest.
Arguments:
- inputs: bfloat16 [2048, 8192], P('ctx', 'head'), may hold values from -6 to 6
- grad_out: bfloat16 [2048, 8192], P('ctx', 'head'), may hold values from -18 to 18
- b_proj: bfloat16 [2048, 128], P('ctx'), may hold values from -0.25 to 0.25
- c_proj: bfloat16 [2048, 128], P('ctx'), may hold values from -0.25 to 0.25
- log_decay: float32 [128, 2048], P('head', 'ctx'), may hold values from -1 to 0, as said below
Outputs:
- grad_x: bfloat16 [2048, 8192], P('ctx', 'head')
- grad_b: float32 [2048, 128], P(('ctx', 'head'))
- grad_c: float32 [2048, 128], P(('ctx', 'head'))
- grad_decay: float32 [128, 2048], P('head', 'ctx')
The draws below stay inside these ranges and needn't reach their ends.
Inputs may be any that keep to these rules, and one draw needn't show every extreme that they name: `log_decay`: log of a decay factor, negative.
All inputs are finite; a program needn't handle non-finite values.
Results may differ from the reference program's by a relative error of at most 0.0057.
Values sent between devices are 32-bit elements; how exact they have to be, the bound alone decides.
No kernel may reach another device: no remote copies, remote signals or barrier semaphores. Data moves between devices by JAX's collectives and lax.ppermute only.
A program may use at most 384 MiB of HBM per device.

```python
import math
import jax
import jax.numpy as jnp
from jax import lax

HEAD_TOTAL = 128
HEAD_DIM = 64
STATE = 128
SPAN = 128
TOKEN_COUNT = 2048


def draw_grad_out(key, part):
    place = jnp.arange(TOKEN_COUNT, dtype=jnp.float32)[:, None] / TOKEN_COUNT
    base = jax.random.truncated_normal(key, -6.0, 6.0, (TOKEN_COUNT, HEAD_TOTAL * HEAD_DIM), jnp.float32)
    rising = 1.0 + 2.0 * place
    return (base * rising).astype(jnp.bfloat16)


def draw_log_decay(key, part):
    random_keys = jax.random.split(jax.random.fold_in(key, 17), 6)
    slow_share = 0.5
    picked = jax.random.uniform(random_keys[0], (HEAD_TOTAL, 1), jnp.float32) < slow_share
    slow_rate = jnp.exp(jax.random.uniform(random_keys[1], (HEAD_TOTAL, 1), jnp.float32, math.log(0.05 / TOKEN_COUNT), math.log(1.0 / TOKEN_COUNT)))
    fast_rate = jnp.exp(jax.random.uniform(random_keys[2], (HEAD_TOTAL, 1), jnp.float32, math.log(1.0 / 50.0), math.log(1.0 / 30.0)))
    decay_speeds = jnp.where(picked, slow_rate, fast_rate)
    coarse_values = jnp.exp(jax.random.uniform(random_keys[3], (HEAD_TOTAL, TOKEN_COUNT), jnp.float32, math.log(0.5), math.log(2.0)))
    spike_sample = jax.random.uniform(random_keys[4], (HEAD_TOTAL, TOKEN_COUNT), jnp.float32)
    spike_length = jnp.log(jax.random.uniform(random_keys[5], (HEAD_TOTAL, TOKEN_COUNT), jnp.float32, 0.5, 0.8))
    spike_events = jnp.where(spike_sample < 2.0 / TOKEN_COUNT, spike_length, 0.0)
    return (-decay_speeds * coarse_values + spike_events).astype(jnp.float32)


def level_of(rng, dims, shards, least, high):
    def one(dim, shards_of):
        heights = jax.random.uniform(jax.random.fold_in(jax.random.fold_in(rng, 6), dim), (shards_of,), jnp.float32, least / len(shards), high / len(shards))
        return jnp.repeat(jnp.exp(heights), dims[dim] // shards_of).reshape((-1,) + (1,) * (len(dims) - dim - 1))

    gain = one(*shards[0])
    for cut in shards[1:]:
        gain = gain * one(*cut)
    return gain


def gaussian(key, dims, deviation, reach, cuts=(), kind=jnp.bfloat16):
    array = jax.random.normal(key, dims, jnp.float32) * deviation
    if len(cuts) > 0:
        array = level_of(key, dims, cuts, -0.22, 0.18) * array
    return jnp.clip(array, min=-reach, max=reach).astype(kind)


def setup_inputs(seed: int = 0) -> dict:
    seeds = jax.random.split(jax.random.key(seed), 6)
    inputs = gaussian(seeds[0], (TOKEN_COUNT, HEAD_TOTAL * HEAD_DIM), 1.0, 6.0, ((0, 8), (1, 4)))
    grad_out = draw_grad_out(jax.random.fold_in(seeds[5], 71), 0)
    b_proj = gaussian(seeds[2], (TOKEN_COUNT, STATE), (4 * STATE) ** -0.5, 0.25, ((0, 8),))
    c_proj = gaussian(seeds[3], (TOKEN_COUNT, STATE), (4 * STATE) ** -0.5, 0.25, ((0, 8),))
    log_decay = draw_log_decay(jax.random.fold_in(seeds[5], 71), 0)
    return {"inputs": inputs, "grad_out": grad_out, "b_proj": b_proj, "c_proj": c_proj, "log_decay": log_decay}


HIGHEST = lax.Precision.HIGHEST


def decay_factors(decay_rows, b_rows, c_rows):
    running = jnp.cumsum(decay_rows, axis=1)
    totals = running[:, -1]
    into_end = jnp.exp(totals[:, None] - running)
    from_start = jnp.exp(running)
    b_decayed = (into_end[:, :, None] * b_rows.astype(jnp.float32)[None]).astype(jnp.bfloat16)
    c_decayed = (from_start[:, :, None] * c_rows.astype(jnp.float32)[None]).astype(jnp.bfloat16)
    return totals, running, into_end, from_start, b_decayed, c_decayed


def mask_table(running):
    length = running.shape[1]
    lower_mask = (jnp.arange(length)[:, None] >= jnp.arange(length)[None, :])[None]
    spread = jnp.where(lower_mask, running[:, :, None] - running[:, None, :], 0.0)
    return jnp.where(lower_mask, jnp.exp(spread), 0.0)


def reference(inputs, grad_out, b_proj, c_proj, log_decay):
    blocks = TOKEN_COUNT // SPAN
    x_all = inputs.reshape(blocks, SPAN, HEAD_TOTAL, HEAD_DIM)
    dy_all = grad_out.reshape(blocks, SPAN, HEAD_TOTAL, HEAD_DIM)
    b_all = b_proj.reshape(blocks, SPAN, STATE)
    c_all = c_proj.reshape(blocks, SPAN, STATE)
    decay_all = log_decay.reshape(HEAD_TOTAL, blocks, SPAN).transpose(1, 0, 2)
    zero_state = jnp.zeros((HEAD_TOTAL, HEAD_DIM, STATE), jnp.float32)

    def forward_step(carry, pieces):
        decay_rows, x_rows, b_rows = pieces
        totals, running, into_end, from_start, b_decayed, c_decayed = decay_factors(decay_rows, b_rows, b_rows)
        local = jnp.einsum("jhp,hjn->hpn", x_rows.astype(jnp.float32), b_decayed.astype(jnp.float32), precision=HIGHEST)
        return jnp.exp(totals)[:, None, None] * carry + local, carry

    def backward_step(carry, pieces):
        decay_rows, dy_rows, c_rows = pieces
        totals, running, into_end, from_start, b_decayed, c_decayed = decay_factors(decay_rows, c_rows, c_rows)
        local = jnp.einsum("ihp,hin->hpn", dy_rows.astype(jnp.float32), c_decayed.astype(jnp.float32), precision=HIGHEST)
        return jnp.exp(totals)[:, None, None] * carry + local, carry

    unused_end, starts = lax.scan(forward_step, zero_state, (decay_all, x_all, b_all))
    unused_begin, ends = lax.scan(backward_step, zero_state, (decay_all, dy_all, c_all), reverse=True)

    def span_grads(pieces):
        decay_rows, x_rows, dy_rows, b_rows, c_rows, start, finish = pieces
        totals, running, into_end, from_start, b_decayed, c_decayed = decay_factors(decay_rows, b_rows, c_rows)
        mask_decay = mask_table(running)
        scores = jnp.dot(c_rows, b_rows.T, preferred_element_type=jnp.float32)
        forward_w = (mask_decay * scores[None]).astype(jnp.bfloat16)
        forward_wide = lax.optimization_barrier(forward_w).astype(jnp.float32)
        x_wide = x_rows.astype(jnp.float32)
        dy_wide = dy_rows.astype(jnp.float32)
        outputs_y = jnp.einsum("hij,jhp->ihp", forward_wide, x_wide, precision=HIGHEST)
        outputs_y = outputs_y + jnp.einsum("hin,hpn->ihp", c_decayed.astype(jnp.float32), start, precision=HIGHEST)
        grad_full = jnp.einsum("hij,ihp->jhp", forward_wide, dy_wide, precision=HIGHEST)
        grad_full = grad_full + jnp.einsum("hjn,hpn->jhp", b_decayed.astype(jnp.float32), finish, precision=HIGHEST)
        pair_grad = jnp.einsum("ihp,jhp->hij", dy_wide, x_wide, precision=HIGHEST)
        weight_grad = (mask_decay * pair_grad).astype(jnp.bfloat16)
        summed = jnp.sum(lax.optimization_barrier(weight_grad).astype(jnp.float32), axis=0)
        dy_scaled = dy_wide * from_start.T[:, :, None]
        x_scaled = x_wide * into_end.T[:, :, None]
        grad_c = jnp.dot(summed, b_rows.astype(jnp.float32), precision=HIGHEST)
        grad_c = grad_c + jnp.einsum("ihp,hpn->in", dy_scaled, start, precision=HIGHEST)
        grad_b = jnp.dot(summed.T, c_rows.astype(jnp.float32), precision=HIGHEST)
        grad_b = grad_b + jnp.einsum("jhp,hpn->jn", x_scaled, finish, precision=HIGHEST)
        change = jnp.einsum("ihp,ihp->hi", dy_wide, outputs_y) - jnp.einsum("jhp,jhp->hj", x_wide, grad_full)
        return grad_full.astype(jnp.bfloat16), grad_b, grad_c, change

    results = lax.map(span_grads, (decay_all, x_all, dy_all, b_all, c_all, starts, ends))
    grad_x = results[0].reshape(TOKEN_COUNT, HEAD_TOTAL * HEAD_DIM)
    grad_b = results[1].reshape(TOKEN_COUNT, STATE)
    grad_c = results[2].reshape(TOKEN_COUNT, STATE)
    change = results[3].transpose(1, 0, 2).reshape(HEAD_TOTAL, TOKEN_COUNT)
    grad_decay = jnp.flip(jnp.cumsum(jnp.flip(change, 1), axis=1), 1)
    return grad_x, grad_b, grad_c, grad_decay
```

```python
import functools

import jax
import jax.numpy as jnp
from jax import lax
from jax.experimental import pallas as pl
from jax.experimental.pallas import tpu as pltpu
from jax.sharding import PartitionSpec as P

HEAD_DIM = 64
STATE = 128
HEADS = 8
WIDE = HEADS * HEAD_DIM
PAIR_FIRST = (True, True, False, False)

F32 = jnp.float32
BF16 = jnp.bfloat16
HIGHEST = lax.Precision.HIGHEST
NN = (((1,), (0,)), ((), ()))
NT = (((1,), (1,)), ((), ()))
TN = (((0,), (0,)), ((), ()))
VMEM_LIMIT = 48 * 1024 * 1024


def dot(a, b, dims=NN):
    return lax.dot_general(a, b, dims, preferred_element_type=F32)


def dot_full(a, b, dims=NN):
    return lax.dot_general(a, b, dims, precision=HIGHEST, preferred_element_type=F32)


def halves(a):
    high = a.astype(BF16)
    return high, (a - high.astype(F32)).astype(BF16)


def dot_halves(a, b, dims=NN):
    high, low = halves(a)
    return dot(high, b, dims) + dot(low, b, dims)


def at_least(shape, row_dim, col_dim):
    return lax.broadcasted_iota(jnp.int32, shape, row_dim) >= lax.broadcasted_iota(
        jnp.int32, shape, col_dim
    )


def spread_matrix(heads):
    shape = (heads, heads * HEAD_DIM)
    lane = lax.broadcasted_iota(jnp.int32, shape, 1)
    first = lax.broadcasted_iota(jnp.int32, shape, 0) * HEAD_DIM
    return jnp.where((lane >= first) & (lane < first + HEAD_DIM), 1.0, 0.0).astype(F32)


def running_rows(decay):
    length = decay.shape[1]
    tri = jnp.where(at_least((length, length), 1, 0), 1.0, 0.0).astype(F32)
    return dot_full(decay, tri)


def running_columns(decay):
    length = decay.shape[1]
    tri = jnp.where(at_least((length, length), 0, 1), 1.0, 0.0).astype(F32)
    return dot_full(tri, decay, NT)


def decay_kernel(decay_ref, out_ref):
    totals = jnp.sum(decay_ref[...], axis=1, keepdims=True)
    heads = totals.shape[0]
    row = jnp.sum(spread_matrix(heads) * totals, axis=0, keepdims=True)
    out_ref[...] = jnp.broadcast_to(jnp.exp(row), out_ref.shape)


def local_kernel(decay_ref, x_ref, dy_ref, b_ref, c_ref, state_ref, adjoint_ref, xs_ref, dys_ref):
    columns = running_columns(decay_ref[...])
    length = columns.shape[0]
    last = columns[length - 1 : length, :]
    spread = spread_matrix(HEADS).astype(BF16)
    into_end = dot_halves(jnp.exp(last - columns), spread)
    from_start = dot_halves(jnp.exp(columns), spread)
    xs = (x_ref[...].astype(F32) * into_end).astype(BF16)
    dys = (dy_ref[...].astype(F32) * from_start).astype(BF16)
    xs_ref[...] = xs
    dys_ref[...] = dys
    state_ref[0] = dot(b_ref[...], xs, TN)
    adjoint_ref[0] = dot(c_ref[...], dys, TN)


def intra_kernel(
    decay_ref, x_ref, dy_ref, b_ref, c_ref, dx_ref, change_ref, gb_ref, gc_ref, table_ref
):
    step = pl.program_id(0)
    decay = decay_ref[...]
    rows = running_rows(decay)
    columns = running_columns(decay)
    length = rows.shape[1]
    b, c = b_ref[...], c_ref[...]
    scores = dot(b, c, NT)
    keep = at_least((length, length), 1, 0)
    half = lax.broadcasted_iota(jnp.int32, (length, 2 * HEAD_DIM), 1) < HEAD_DIM
    total = jnp.zeros((length, length), F32)
    for pair in range(HEADS // 2):
        lanes = slice(pair * 2 * HEAD_DIM, (pair + 1) * 2 * HEAD_DIM)
        x2 = x_ref[:, lanes]
        dy2 = dy_ref[:, lanes]
        parts = []
        for side in range(2):
            head = 2 * pair + side
            own = half if side == 0 else jnp.logical_not(half)
            x1 = jnp.where(own, x2.astype(F32), 0.0).astype(BF16)
            pairs = dot(x1, dy2, NT)
            gap = rows[head : head + 1, :] - columns[:, head : head + 1]
            mask = jnp.exp(jnp.where(keep, gap, -1e30))
            weights = (mask * scores).astype(BF16)
            total = total + mask * pairs
            change_ref[head : head + 1, :] = jnp.sum(
                weights.astype(F32) * pairs, axis=0, keepdims=True
            )
            parts.append(dot(weights, dy2))
        dx_ref[:, lanes] = jnp.where(half, parts[0], parts[1])

    @pl.when(step == 0)
    def _():
        table_ref[...] = total

    @pl.when(step > 0)
    def _():
        table_ref[...] += total

    @pl.when(step == pl.num_programs(0) - 1)
    def _():
        table = table_ref[...]
        gb_ref[...] = dot_halves(table, c)
        gc_ref[...] = dot_halves(table, b, TN)


def inter_kernel(
    decay_ref,
    state_in_ref,
    adjoint_in_ref,
    state_ref,
    total_ref,
    x_ref,
    xs_ref,
    dys_ref,
    b_ref,
    c_ref,
    dx_ref,
    change_ref,
    gb_ref,
    gc_ref,
    gx_ref,
    gd_ref,
    gb_out_ref,
    gc_out_ref,
):
    columns = running_columns(decay_ref[...])
    length = columns.shape[0]
    last = columns[length - 1 : length, :]
    spread = spread_matrix(HEADS).astype(BF16)
    into_end = dot_halves(jnp.exp(last - columns), spread)
    state_in = state_in_ref[...]
    adjoint_in = adjoint_in_ref[...]
    state_low = state_in.astype(BF16)
    adjoint_low = adjoint_in.astype(BF16)
    xs = xs_ref[...]
    dys = dys_ref[...]
    gb_out_ref[...] = gb_ref[...] + dot(xs, adjoint_low, NT)
    gc_out_ref[...] = gc_ref[...] + dot(dys, state_low, NT)
    grad_full = dx_ref[...] + into_end * dot(b_ref[...], adjoint_low)
    gx_ref[...] = grad_full.astype(BF16)
    change = dys.astype(F32) * dot(c_ref[...], state_low) - x_ref[...].astype(F32) * grad_full
    high, low = halves(change)
    per_head = change_ref[...] + dot(spread, high, NT) + dot(spread, low, NT)
    after = jnp.where(at_least((length, length), 0, 1), 1.0, 0.0).astype(F32)
    suffix = dot_full(per_head, after)
    state_end = total_ref[0:1, :] * state_in + state_ref[0]
    high, low = halves(state_end * adjoint_in)
    later = dot(spread, high, NT) + dot(spread, low, NT)
    gd_ref[...] = suffix + jnp.sum(later, axis=1, keepdims=True)


def params():
    return pltpu.CompilerParams(vmem_limit_bytes=VMEM_LIMIT)


def cost(flops, nbytes):
    return pl.CostEstimate(flops=flops, bytes_accessed=nbytes, transcendentals=0)


def whole(shape):
    return pl.BlockSpec(shape, lambda k: (0,) * len(shape))


def decay_totals(log_decay):
    heads = log_decay.shape[0]
    return pl.pallas_call(
        decay_kernel,
        out_shape=jax.ShapeDtypeStruct((8, heads * HEAD_DIM), F32),
        name="decay_totals",
    )(log_decay)


def local_states(log_decay, x, dy, b, c):
    tokens, width = x.shape
    chunks = width // WIDE
    wide = pl.BlockSpec((tokens, WIDE), lambda k: (0, k))
    rows = pl.BlockSpec((HEADS, tokens), lambda k: (k, 0))
    proj = whole((tokens, STATE))
    states = pl.BlockSpec((1, STATE, WIDE), lambda k: (k, 0, 0))
    return pl.pallas_call(
        local_kernel,
        grid=(chunks,),
        in_specs=[rows, wide, wide, proj, proj],
        out_specs=[states, states, wide, wide],
        out_shape=[
            jax.ShapeDtypeStruct((chunks, STATE, WIDE), F32),
            jax.ShapeDtypeStruct((chunks, STATE, WIDE), F32),
            jax.ShapeDtypeStruct((tokens, width), BF16),
            jax.ShapeDtypeStruct((tokens, width), BF16),
        ],
        compiler_params=params(),
        cost_estimate=cost(4 * tokens * STATE * width, 12 * tokens * width),
        name="local_states",
    )(log_decay, x, dy, b, c)


def intra(log_decay, x, dy, b, c):
    tokens, width = x.shape
    chunks = width // WIDE
    wide = pl.BlockSpec((tokens, WIDE), lambda k: (0, k))
    rows = pl.BlockSpec((HEADS, tokens), lambda k: (k, 0))
    proj = whole((tokens, STATE))
    return pl.pallas_call(
        intra_kernel,
        grid=(chunks,),
        in_specs=[rows, wide, wide, proj, proj],
        out_specs=[wide, rows, proj, proj],
        out_shape=[
            jax.ShapeDtypeStruct((tokens, width), F32),
            jax.ShapeDtypeStruct(log_decay.shape, F32),
            jax.ShapeDtypeStruct((tokens, STATE), F32),
            jax.ShapeDtypeStruct((tokens, STATE), F32),
        ],
        scratch_shapes=[pltpu.VMEM((tokens, tokens), F32)],
        compiler_params=params(),
        cost_estimate=cost(4 * tokens * tokens * width, 8 * tokens * width),
        name="intra",
    )(log_decay, x, dy, b, c)


def inter(
    chunk, log_decay, state_in, adjoint_in, states, totals, x, xs, dys, b, c, dx, change, gb, gc
):
    tokens = x.shape[0]
    wide = pl.BlockSpec((tokens, WIDE), lambda k: (0, chunk))
    rows = pl.BlockSpec((HEADS, tokens), lambda k: (chunk, 0))
    proj = whole((tokens, STATE))
    return pl.pallas_call(
        inter_kernel,
        grid=(1,),
        in_specs=[
            rows,
            whole((STATE, WIDE)),
            whole((STATE, WIDE)),
            pl.BlockSpec((1, STATE, WIDE), lambda k: (chunk, 0, 0)),
            pl.BlockSpec((8, WIDE), lambda k: (0, chunk)),
            wide,
            wide,
            wide,
            proj,
            proj,
            wide,
            rows,
            proj,
            proj,
        ],
        out_specs=[whole((tokens, WIDE)), whole((HEADS, tokens)), proj, proj],
        out_shape=[
            jax.ShapeDtypeStruct((tokens, WIDE), BF16),
            jax.ShapeDtypeStruct((HEADS, tokens), F32),
            jax.ShapeDtypeStruct((tokens, STATE), F32),
            jax.ShapeDtypeStruct((tokens, STATE), F32),
        ],
        compiler_params=params(),
        cost_estimate=cost(8 * tokens * STATE * WIDE, 16 * tokens * WIDE),
        name="inter",
    )(log_decay, state_in, adjoint_in, states, totals, x, xs, dys, b, c, dx, change, gb, gc)


def group_rounds(groups):
    rounds = []
    span = 1
    while span < groups:
        permutes = []
        for step in range(span):
            links = []
            for first in range(0, groups, 2 * span):
                links.append((first + span - 1, first + span + step))
                links.append((first + span, first + span - 1 - step))
            permutes.append([(s, t) for s, t in links if s < groups and t < groups])
        rounds.append((span, permutes))
        span *= 2
    return rounds


def group_scan(forward, backward, total, group, groups):
    carried_f = carried_b = None
    decay_f = decay_b = jnp.ones_like(total)
    rounds = group_rounds(groups)
    for number, (span, permutes) in enumerate(rounds):
        upper = (group // span) % 2 == 1
        if carried_f is None:
            send = jnp.where(upper, backward, forward)
        else:
            send = jnp.where(
                upper, total * carried_b + backward, total * carried_f + forward
            )
        more = number + 1 < len(rounds)
        if more:
            decay = total * jnp.where(upper, decay_b, decay_f)
            send = jnp.concatenate([send, jnp.broadcast_to(decay, (8, send.shape[1]))], axis=0)
        got = None
        for links in permutes:
            both = [(2 * s + side, 2 * t + side) for s, t in links for side in range(2)]
            part = lax.ppermute(send, "ctx", both)
            got = part if got is None else got + part
        value = got[:STATE]
        if carried_f is None:
            carried_f = jnp.where(upper, value, 0.0)
            carried_b = jnp.where(upper, 0.0, value)
        else:
            carried_f = jnp.where(upper, decay_f * value + carried_f, carried_f)
            carried_b = jnp.where(upper, carried_b, decay_b * value + carried_b)
        if more:
            seen = got[STATE : STATE + 1]
            decay_f = jnp.where(upper, decay_f * seen, decay_f)
            decay_b = jnp.where(upper, decay_b, decay_b * seen)
    if carried_f is None:
        return jnp.zeros_like(forward), jnp.zeros_like(backward)
    return carried_f, carried_b


def shards(inputs, grad_out, b_proj, c_proj, log_decay):
    count = lax.axis_size("ctx")
    mine = lax.axis_index("ctx")
    second = mine % 2 == 1
    group, groups = mine // 2, count // 2
    swap = [(i, i ^ 1) for i in range(count)]

    totals = decay_totals(log_decay)
    other_totals = lax.ppermute(totals[0:1], "ctx", swap)
    states, adjoints, xs, dys = local_states(log_decay, inputs, grad_out, b_proj, c_proj)
    chunks = states.shape[0]
    entering = [None] * chunks
    for k in range(chunks):
        state, adjoint = states[k], adjoints[k]
        own = totals[0:1, k * WIDE : (k + 1) * WIDE]
        other = other_totals[0:1, k * WIDE : (k + 1) * WIDE]
        both = own * other
        if PAIR_FIRST[k % len(PAIR_FIRST)]:
            got = lax.ppermute(jnp.concatenate([state, adjoint], axis=0), "ctx", swap)
            state_p, adjoint_p = got[:STATE], got[STATE:]
            forward = jnp.where(second, own * state_p + state, other * state + state_p)
            backward = jnp.where(second, adjoint_p + other * adjoint, adjoint + own * adjoint_p)
            carried_f, carried_b = group_scan(forward, backward, both, group, groups)
            entering[k] = (
                jnp.where(second, other * carried_f + state_p, carried_f),
                jnp.where(second, carried_b, other * carried_b + adjoint_p),
            )
        else:
            forward = jnp.where(second, state, other * state)
            backward = jnp.where(second, other * adjoint, adjoint)
            carried_f, carried_b = group_scan(forward, backward, both, group, groups)
            send_f = jnp.where(second, carried_f, own * carried_f + state)
            send_b = jnp.where(second, own * carried_b + adjoint, carried_b)
            got = lax.ppermute(jnp.concatenate([send_f, send_b], axis=0), "ctx", swap)
            entering[k] = (
                jnp.where(second, other * carried_f, carried_f) + got[:STATE],
                jnp.where(second, carried_b, other * carried_b) + got[STATE:],
            )

    dx, change, gb, gc = intra(log_decay, inputs, grad_out, b_proj, c_proj)
    order = [k for i in range(chunks) for k in range(chunks) if k % 2 * 2 + k // 2 == i]
    parts_x, parts_d = [None] * chunks, [None] * chunks
    for k in order if chunks == 4 else range(chunks):
        parts_x[k], parts_d[k], gb, gc = inter(
            k, log_decay, *entering[k], states, totals, inputs, xs, dys, b_proj, c_proj,
            dx, change, gb, gc,
        )
    grad_x = jnp.concatenate(parts_x, axis=1)
    grad_decay = jnp.concatenate(parts_d, axis=0)

    ranks = lax.axis_size("head")
    rank = lax.axis_index("head")
    rows = gb.shape[0] // ranks
    sums = jnp.stack([gb, gc])

    def piece(owner):
        return lax.dynamic_slice_in_dim(sums, owner * rows, rows, axis=1)

    result = piece(rank)
    for step in range(1, ranks):
        links = [(i, i ^ step) for i in range(ranks)]
        result = result + lax.ppermute(piece(rank ^ step), "head", links)
    return grad_x, result[0], result[1], grad_decay


def solution(mesh):
    placed = (P("ctx", "head"), P("ctx", "head"), P("ctx", None), P("ctx", None), P("head", "ctx"))
    return jax.shard_map(
        shards,
        mesh=mesh,
        in_specs=placed,
        out_specs=(
            P("ctx", "head"),
            P(("ctx", "head"), None),
            P(("ctx", "head"), None),
            P("head", "ctx"),
        ),
        check_vma=False,
    )
```

```python
import functools

import jax
import jax.numpy as jnp
from jax import lax
from jax.experimental import pallas as pl
from jax.experimental.pallas import tpu as pltpu
from jax.sharding import PartitionSpec as P

HEAD_DIM = 64
STATE = 128
HEADS = 8
WIDE = HEADS * HEAD_DIM

F32 = jnp.float32
BF16 = jnp.bfloat16
HIGHEST = lax.Precision.HIGHEST
NN = (((1,), (0,)), ((), ()))
NT = (((1,), (1,)), ((), ()))
TN = (((0,), (0,)), ((), ()))
VMEM_LIMIT = 16 * 1024 * 1024
VMEM_ALL = 61 * 1024 * 1024


def dot(a, b, dims=NN):
    return lax.dot_general(a, b, dims, preferred_element_type=F32)


def dot_full(a, b, dims=NN):
    return lax.dot_general(a, b, dims, precision=HIGHEST, preferred_element_type=F32)


def halves(a):
    high = a.astype(BF16)
    return high, (a - high.astype(F32)).astype(BF16)


def dot_halves(a, b, dims=NN):
    high, low = halves(a)
    return dot(high, b, dims) + dot(low, b, dims)


def at_least(shape, row_dim, col_dim):
    return lax.broadcasted_iota(jnp.int32, shape, row_dim) >= lax.broadcasted_iota(
        jnp.int32, shape, col_dim
    )


def spread_matrix(heads):
    shape = (heads, heads * HEAD_DIM)
    lane = lax.broadcasted_iota(jnp.int32, shape, 1)
    first = lax.broadcasted_iota(jnp.int32, shape, 0) * HEAD_DIM
    return jnp.where((lane >= first) & (lane < first + HEAD_DIM), 1.0, 0.0).astype(F32)


def lower_ones(length, row_dim, col_dim):
    return jnp.where(at_least((length, length), row_dim, col_dim), 1.0, 0.0).astype(F32)


def per_head(values):
    spread = spread_matrix(values.shape[1] // HEAD_DIM).astype(BF16)
    high, low = halves(values)
    return dot(spread, high, NT) + dot(spread, low, NT)


def first_half(rows):
    return lax.broadcasted_iota(jnp.int32, (rows, 2 * HEAD_DIM), 1) < HEAD_DIM


def over_lanes(columns):
    rows, heads = columns.shape
    half = first_half(rows)
    parts = []
    for head in range(0, heads, 2):
        left = jnp.broadcast_to(columns[:, head : head + 1], half.shape)
        right = jnp.broadcast_to(columns[:, head + 1 : head + 2], half.shape)
        parts.append(jnp.where(half, left, right))
    return jnp.concatenate(parts, axis=1)


def local_kernel(groups, decay_in, x_in, dy_in, b_in, c_in, *refs):
    chunks = x_in.shape[1] // WIDE
    late = chunks // 2
    count = 5 + chunks + late
    outs = refs[:count]
    decay_ref, x_ref, dy_ref, b_ref, c_ref = refs[count : count + 5]
    kept = refs[count + 5 : count + 10]
    rows_ref, columns_ref, into_ref, from_ref, totals_ref = kept
    messages, sends, small_sem, wide_sem, out_sem = refs[count + 10 :]
    pending = []

    def leave(source, target):
        copy = pltpu.make_async_copy(source, target, out_sem.at[len(pending)])
        copy.start()
        pending.append(copy)

    small = [
        pltpu.make_async_copy(source, target, small_sem.at[i])
        for i, (source, target) in enumerate(((decay_in, decay_ref), (b_in, b_ref), (c_in, c_ref)))
    ]
    wide = []
    for chunk in range(chunks):
        lanes = pl.ds(chunk * WIDE, WIDE)
        wide.append(
            [
                pltpu.make_async_copy(source.at[:, lanes], target.at[:, lanes], wide_sem.at[i, chunk])
                for i, (source, target) in enumerate(((x_in, x_ref), (dy_in, dy_ref)))
            ]
        )
    for copy in small + [copy for pair in wide for copy in pair]:
        copy.start()
    last_group = lax.axis_index("ctx") // 2 == groups - 1
    small[0].wait()
    length = decay_ref.shape[1]
    rows = dot_full(decay_ref[...], lower_ones(length, 1, 0))
    rows_ref[...] = rows
    columns_ref[...] = rows.T
    into_end = jnp.exp(rows[:, length - 1 : length] - rows)
    from_start = jnp.exp(rows)
    into_ref[...] = into_end.T
    from_column = from_start.T
    from_ref[...] = from_column
    small[1].wait()
    small[2].wait()
    b_t = b_ref[...].astype(F32).T
    c_t = c_ref[...].astype(F32).T
    half = first_half(STATE)

    def gathered(proj, factors, values_ref, pair):
        head = 2 * pair
        scaled = jnp.concatenate(
            [proj * factors[head : head + 1, :], proj * factors[head + 1 : head + 2, :]], axis=0
        )
        sums = dot(scaled.astype(BF16), values_ref[:, pl.ds(pair * STATE, STATE)])
        return jnp.where(half, sums[:STATE], sums[STATE:])

    for chunk in range(chunks):
        lanes = pl.ds(chunk * WIDE, WIDE)
        heads = slice(chunk * HEADS, (chunk + 1) * HEADS)
        pairs = range(chunk * HEADS // 2, (chunk + 1) * HEADS // 2)
        totals_ref[:, lanes] = over_lanes(from_column[length - 8 :, heads])[7:8, :]
        for place, (proj, factors, values_ref, rows_at) in enumerate(
            ((b_t, into_end, x_ref, 0), (c_t, from_start, dy_ref, STATE))
        ):
            wide[chunk][place].wait()
            for pair in pairs:
                at = (pair - pairs[0]) * STATE
                messages[chunk, rows_at : rows_at + STATE, at : at + STATE] = gathered(
                    proj, factors, values_ref, pair
                )
        leave(messages.at[chunk], outs[5 + chunk])
        if chunk >= chunks - late:
            sends[chunk - chunks + late] = jnp.where(
                last_group, messages[chunk, STATE:, :], messages[chunk, :STATE, :]
            )
            leave(sends.at[chunk - chunks + late], outs[5 + late + chunk])
    for source, target in zip(kept, outs[:5]):
        leave(source, target)
    for copy in pending:
        copy.wait()


def intra_kernel(
    chunk,
    rows_ref,
    columns_ref,
    into_ref,
    from_ref,
    x_ref,
    dy_ref,
    b_ref,
    c_ref,
    dx_ref,
    xs_ref,
    dys_ref,
    change_ref,
    gb_ref,
    gc_ref,
    table_ref,
):
    rows = rows_ref[...]
    heads = slice(chunk * HEADS, (chunk + 1) * HEADS)
    columns = columns_ref[:, heads]
    xs_ref[...] = (x_ref[...].astype(F32) * over_lanes(into_ref[:, heads])).astype(BF16)
    dys_ref[...] = (dy_ref[...].astype(F32) * over_lanes(from_ref[:, heads])).astype(BF16)
    length = rows.shape[1]
    b, c = b_ref[...], c_ref[...]
    scores = dot(b, c, NT)
    size = STATE
    keep = at_least((size, size), 1, 0)
    half = first_half(size)
    blocks = length // size

    table_ref[...] = jnp.zeros_like(table_ref)

    for pair in range(HEADS // 2):
        lanes = slice(pair * 2 * HEAD_DIM, (pair + 1) * 2 * HEAD_DIM)
        dy2 = dy_ref[:, lanes]
        sums = [None, None]
        for block in range(blocks):
            first = block * size
            x2 = x_ref[first : first + size, lanes].astype(F32)
            parts = []
            for side in range(2):
                head = 2 * pair + side
                own = half if side == 0 else jnp.logical_not(half)
                x1 = jnp.where(own, x2, 0.0).astype(BF16)
                pairs = dot(x1, dy2[first:], NT)
                gap = rows[head : head + 1, first:] - columns[first : first + size, head : head + 1]
                near = jnp.where(keep, gap[:, :size], -1e30)
                if length - first > size:
                    near = jnp.concatenate([near, gap[:, size:]], axis=1)
                mask = jnp.exp(near)
                weights = (mask * scores[first : first + size, first:]).astype(BF16)
                table_ref[first : first + size, first:] += mask * pairs
                change = jnp.sum(weights.astype(F32) * pairs, axis=0, keepdims=True)
                if block == 0:
                    sums[side] = change
                else:
                    sums[side] = jnp.concatenate(
                        [sums[side][:, :first], sums[side][:, first:] + change], axis=1
                    )
                parts.append(dot(weights, dy2[first:]))
            dx_ref[first : first + size, lanes] = jnp.where(half, parts[0], parts[1])
        for side in range(2):
            head = 2 * pair + side
            change_ref[head : head + 1, :] = sums[side]

    change_ref[...] -= per_head(x_ref[...].astype(F32) * dx_ref[...])
    table = table_ref[...]
    gb_ref[...] = dot_halves(table, c)
    gc_ref[...] = dot_halves(table, b, TN)


def inter_kernel(
    chunk,
    into_ref,
    state_in_ref,
    adjoint_in_ref,
    total_ref,
    xs_ref,
    dys_ref,
    b_ref,
    c_ref,
    dx_ref,
    gb_ref,
    gc_ref,
    gx_ref,
    change_ref,
    earlier_ref,
    later_ref,
    gb_out_ref,
    gc_out_ref,
):
    lanes = slice(chunk * WIDE, (chunk + 1) * WIDE)
    heads = slice(chunk * HEADS, (chunk + 1) * HEADS)
    state_in = state_in_ref[...]
    adjoint_in = adjoint_in_ref[...]
    state_low = state_in.astype(BF16)
    adjoint_low = adjoint_in.astype(BF16)
    xs = xs_ref[...]
    dys = dys_ref[...]
    gb_out_ref[...] = gb_ref[...] + dot(xs, adjoint_low, NT)
    gc_out_ref[...] = gc_ref[...] + dot(dys, state_low, NT)
    outer = dot(b_ref[...], adjoint_low)
    gx_ref[...] = (dx_ref[...] + over_lanes(into_ref[:, heads]) * outer).astype(BF16)
    change_ref[...] = per_head(dys.astype(F32) * dot(c_ref[...], state_low))
    earlier_ref[...] = per_head(xs.astype(F32) * outer)
    later_ref[...] = per_head(total_ref[:, lanes] * state_in * adjoint_in)


def suffix_kernel(chunks, *refs):
    out_ref = refs[-1]
    length = out_ref.shape[1]

    def joined(place):
        return jnp.concatenate([ref[...] for ref in refs[place * chunks : (place + 1) * chunks]], 0)

    from_here = dot_full(joined(0) + joined(1), lower_ones(length, 0, 1))
    before = dot_full(joined(2), 1.0 - lower_ones(length, 0, 1))
    out_ref[...] = from_here + before + jnp.sum(joined(3), axis=1, keepdims=True)


def params(limit=VMEM_LIMIT):
    return pltpu.CompilerParams(vmem_limit_bytes=limit)


def cost(flops, nbytes):
    return pl.CostEstimate(flops=flops, bytes_accessed=nbytes, transcendentals=0)


def shape(dims, dtype=F32):
    return jax.ShapeDtypeStruct(dims, dtype)


def vmem(count):
    return [pl.BlockSpec(memory_space=pltpu.VMEM)] * count


def local_states(groups, log_decay, x, dy, b, c):
    tokens, width = x.shape
    heads = log_decay.shape[0]
    chunks = width // WIDE
    kept = [(heads, tokens)] + [(tokens, heads)] * 3 + [(1, width)]
    late = chunks // 2
    outs = kept + [(2 * STATE, WIDE)] * chunks + [(STATE, WIDE)] * late
    hbm = pl.BlockSpec(memory_space=pltpu.HBM)
    outs = pl.pallas_call(
        functools.partial(local_kernel, groups),
        in_specs=[hbm] * 5,
        out_specs=[hbm] * len(outs),
        out_shape=[shape(dims) for dims in outs],
        scratch_shapes=[
            pltpu.VMEM(log_decay.shape, F32),
            pltpu.VMEM(x.shape, BF16),
            pltpu.VMEM(x.shape, BF16),
            pltpu.VMEM(b.shape, BF16),
            pltpu.VMEM(b.shape, BF16),
            *[pltpu.VMEM(dims, F32) for dims in kept],
            pltpu.VMEM((chunks, 2 * STATE, WIDE), F32),
            pltpu.VMEM((late, STATE, WIDE), F32),
            pltpu.SemaphoreType.DMA((3,)),
            pltpu.SemaphoreType.DMA((2, chunks)),
            pltpu.SemaphoreType.DMA((len(outs),)),
        ],
        compiler_params=params(VMEM_ALL),
        cost_estimate=cost(4 * tokens * STATE * width, 12 * tokens * width),
        name="local_states",
    )(log_decay, x, dy, b, c)
    return outs[:5], outs[5 : 5 + chunks], [None] * (chunks - late) + list(outs[5 + chunks :])


def intra(chunk, rows, columns, into, start, x, dy, b, c):
    tokens = x.shape[0]
    wide = pl.BlockSpec((tokens, WIDE), lambda k: (0, chunk))
    proj = pl.BlockSpec((tokens, STATE), lambda k: (0, 0))
    return pl.pallas_call(
        functools.partial(intra_kernel, chunk),
        grid=(1,),
        in_specs=[
            pl.BlockSpec((HEADS, tokens), lambda k: (chunk, 0)),
            *[pl.BlockSpec(columns.shape, lambda k: (0, 0))] * 3,
            wide,
            wide,
            proj,
            proj,
        ],
        out_specs=[
            *[pl.BlockSpec((tokens, WIDE), lambda k: (0, 0))] * 3,
            pl.BlockSpec((HEADS, tokens), lambda k: (0, 0)),
            proj,
            proj,
        ],
        out_shape=[
            shape((tokens, WIDE)),
            shape((tokens, WIDE), BF16),
            shape((tokens, WIDE), BF16),
            shape((HEADS, tokens)),
            shape((tokens, STATE)),
            shape((tokens, STATE)),
        ],
        scratch_shapes=[pltpu.VMEM((tokens, tokens), F32)],
        compiler_params=params(),
        cost_estimate=cost(4 * tokens * tokens * WIDE, 8 * tokens * WIDE),
        name="intra",
    )(rows, columns, into, start, x, dy, b, c)


def inter(chunk, into, state_in, adjoint_in, totals, xs, dys, b, c, dx, gb, gc):
    tokens = xs.shape[0]
    args = (into, state_in, adjoint_in, totals, xs, dys, b, c, dx, gb, gc)
    out_shape = [
        shape((tokens, WIDE), BF16),
        shape((HEADS, tokens)),
        shape((HEADS, tokens)),
        shape((HEADS, STATE)),
        shape((tokens, STATE)),
        shape((tokens, STATE)),
    ]
    return pl.pallas_call(
        functools.partial(inter_kernel, chunk),
        in_specs=vmem(len(args)),
        out_specs=vmem(len(out_shape)),
        out_shape=out_shape,
        compiler_params=params(),
        cost_estimate=cost(8 * tokens * STATE * WIDE, 16 * tokens * WIDE),
        name="inter",
    )(*args)


def suffix_sums(*parts):
    chunks = len(parts[0])
    args = [item for part in parts for item in part]
    return pl.pallas_call(
        functools.partial(suffix_kernel, chunks),
        in_specs=vmem(len(args)),
        out_specs=vmem(1)[0],
        out_shape=shape((chunks * HEADS, args[0].shape[1])),
        compiler_params=params(),
        cost_estimate=cost(0, 1 << 17),
        name="suffix_sums",
    )(*args)


class Chunk:
    def __init__(self, first, message, own, other, diagonal, second):
        self.first, self.own, self.other, self.second = first, own, other, second
        self.state, self.adjoint = message[:STATE], message[STATE:]
        both = own * other
        if first:
            self.step_f = self.step_b = both
            self.seen_f = self.seen_b = jnp.ones_like(own)
        else:
            self.forward, self.backward = self.state, self.adjoint
            self.step_f, self.step_b = jnp.where(second, both, own), jnp.where(second, own, both)
            self.seen_f = jnp.where(second, 1.0, diagonal)
            self.seen_b = jnp.where(second, diagonal, 1.0)

    def joined(self, got):
        self.got_f, self.got_b = got[:STATE], got[STATE:]
        own, other = self.own, self.other
        self.forward = jnp.where(
            self.second, own * self.got_f + self.state, other * self.state + self.got_f
        )
        self.backward = jnp.where(
            self.second, self.got_b + other * self.adjoint, self.adjoint + own * self.got_b
        )

    def leaving_f(self, carried):
        return self.step_f * carried + self.forward

    def leaving_b(self, carried):
        return self.step_b * carried + self.backward

    def message(self):
        send_f = jnp.where(self.second, self.in_f, self.own * self.in_f + self.state)
        send_b = jnp.where(self.second, self.own * self.in_b + self.adjoint, self.in_b)
        return jnp.concatenate([send_f, send_b], axis=0)

    def entering(self, got=None):
        decayed_f = jnp.where(self.second, self.other, 1.0) * self.in_f
        decayed_b = jnp.where(self.second, 1.0, self.other) * self.in_b
        if got is not None:
            return decayed_f + got[:STATE], decayed_b + got[STATE:]
        return (
            decayed_f + jnp.where(self.second, self.got_f, 0.0),
            decayed_b + jnp.where(self.second, 0.0, self.got_b),
        )


def between(links):
    return [(2 * s + side, 2 * t + side) for s, t in links for side in range(2)]


def group_scan(chunk, group, groups):
    carried_f, carried_b = jnp.zeros_like(chunk.forward), jnp.zeros_like(chunk.backward)
    for hop in range(1, groups):
        send = jnp.where(
            group == groups - hop, chunk.leaving_b(carried_b), chunk.leaving_f(carried_f)
        )
        links = [(hop - 1, hop), (groups - hop, groups - hop - 1)]
        got = lax.ppermute(send, "ctx", between(links))
        carried_f = jnp.where(group == hop, chunk.seen_f * got, carried_f)
        carried_b = jnp.where(group == groups - hop - 1, chunk.seen_b * got, carried_b)
    chunk.in_f, chunk.in_b = carried_f, carried_b


class Four:
    def __init__(self, group):
        self.lower = group < 2
        self.inner = (group == 1) | (group == 2)

    def first(self, chunk):
        return jnp.where(self.lower, chunk.forward, chunk.backward)

    def second(self, chunk, got):
        chunk.hop1 = got
        scale = jnp.where(self.lower, chunk.step_f * chunk.seen_f, chunk.step_b * chunk.seen_b)
        return scale * got + jnp.where(self.lower, chunk.forward, chunk.backward)

    def third(self, chunk, got):
        chunk.hop2 = got
        scale = jnp.where(self.lower, chunk.step_b * chunk.seen_b, chunk.step_f * chunk.seen_f)
        return scale * got + jnp.where(self.lower, chunk.backward, chunk.forward)

    def done(self, chunk, got):
        near = jnp.where(self.inner, chunk.hop1, 0.0)
        far = jnp.where(self.inner, chunk.hop2, got)
        chunk.in_f = chunk.seen_f * jnp.where(self.lower, near, far)
        chunk.in_b = chunk.seen_b * jnp.where(self.lower, far, near)


def fence(*items):
    return lax.optimization_barrier(items)


def shards(inputs, grad_out, b_proj, c_proj, log_decay):
    count = lax.axis_size("ctx")
    mine = lax.axis_index("ctx")
    second = mine % 2 == 1
    group, groups = mine // 2, count // 2

    def permute(value, links):
        return lax.ppermute(value, "ctx", links)

    swap = [(i, i ^ 1) for i in range(count)]
    diagonals = [(2 * g + 1, 2 * g + 2) for g in range(groups - 1)]
    diagonals += [(t, s) for s, t in diagonals]

    (rows, columns, into, start, totals), messages, sends = local_states(
        groups, log_decay, inputs, grad_out, b_proj, c_proj
    )
    chunks = len(messages)
    other = permute(totals, swap)
    diagonal = permute(totals, diagonals)

    def chunk_of(k, first, message, other, diagonal):
        lanes = slice(k * WIDE, (k + 1) * WIDE)
        return Chunk(
            first, message, totals[:, lanes], other[:, lanes], diagonal[:, lanes], second
        )

    def local(k, rows, columns):
        return intra(k, rows, columns, into, start, inputs, grad_out, b_proj, c_proj)

    def carried(k, entering, near, gb, gc):
        dx, xs, dys = near[:3]
        return inter(k, into, *entering, totals, xs, dys, b_proj, c_proj, dx, gb, gc)

    near, far = [None] * chunks, [None] * chunks
    if groups == 4 and chunks == 4:
        four = Four(group)
        middle = between([(1, 2), (2, 1)])
        sides = between([(0, 1), (1, 0), (2, 3), (3, 2)])

        pair0 = permute(messages[0], swap)
        hop = permute(sends[2], sides)
        other, diagonal, hop, message1, send3, rows, columns = fence(
            other, diagonal, hop, messages[1], sends[3], rows, columns
        )
        c0 = chunk_of(0, True, messages[0], other, diagonal)
        c1 = chunk_of(1, True, message1, other, diagonal)
        c2 = chunk_of(2, False, messages[2], other, diagonal)
        c3 = chunk_of(3, False, messages[3], other, diagonal)

        mid = permute(four.second(c2, hop), middle)
        hop = permute(send3, sides)
        pair1 = permute(message1, swap)
        mid, hop, pair0, rows, columns = fence(mid, hop, pair0, rows, columns)
        c0.joined(pair0)

        side = permute(jnp.where(four.inner, four.third(c2, mid), four.first(c0)), sides)
        mid = permute(four.second(c3, hop), middle)
        near[0], near[1] = local(0, rows, columns), local(1, rows, columns)
        side, mid, pair1, near[0], near[1], rows = fence(side, mid, pair1, near[0], near[1], rows)
        four.done(c2, side)
        c1.joined(pair1)

        pair2 = permute(c2.message(), swap)
        hop = side
        side = permute(jnp.where(four.inner, four.third(c3, mid), four.first(c1)), sides)
        mid = permute(four.second(c0, hop), middle)
        near[2] = local(2, rows, columns)
        side, mid, near[2], rows = fence(side, mid, near[2], rows)
        four.done(c3, side)

        pair3 = permute(c3.message(), swap)
        hop = side
        side = permute(four.third(c0, mid), sides)
        mid = permute(four.second(c1, hop), middle)
        near[3] = local(3, rows, columns)
        gb = sum(item[4] for item in near)
        gc = sum(item[5] for item in near)
        side, mid, pair2, gb, gc = fence(side, mid, pair2, gb, gc)
        four.done(c0, side)

        side = permute(four.third(c1, mid), sides)
        *far[0], gb, gc = carried(0, c0.entering(), near[0], gb, gc)
        *far[2], gb, gc = carried(2, c2.entering(pair2), near[2], gb, gc)
        side, pair3, far[0], far[2], gb, gc = fence(side, pair3, far[0], far[2], gb, gc)
        four.done(c1, side)

        *far[1], gb, gc = carried(1, c1.entering(), near[1], gb, gc)
        *far[3], gb, gc = carried(3, c3.entering(pair3), near[3], gb, gc)
    else:
        near = [local(k, rows, columns) for k in range(chunks)]
        gb = sum(item[4] for item in near)
        gc = sum(item[5] for item in near)
        for k in range(chunks):
            first = k < chunks // 2
            chunk = chunk_of(k, first, messages[k], other, diagonal)
            if first:
                chunk.joined(permute(messages[k], swap))
            group_scan(chunk, group, groups)
            got = None if first else permute(chunk.message(), swap)
            *far[k], gb, gc = carried(k, chunk.entering(got), near[k], gb, gc)
    grad_x = jnp.concatenate([item[0] for item in far], axis=1)
    grad_decay = suffix_sums(
        [item[3] for item in near], *([item[i] for item in far] for i in (1, 2, 3))
    )

    ranks = lax.axis_size("head")
    rank = lax.axis_index("head")
    size = gb.shape[0] // ranks
    sums = jnp.stack([gb, gc])

    def piece(owner):
        return lax.dynamic_slice_in_dim(sums, owner * size, size, axis=1)

    parts = [piece(rank)]
    for step in range(1, ranks):
        links = [(i, i ^ step) for i in range(ranks)]
        parts.append(lax.ppermute(piece(rank ^ step), "head", links))
    grad_b, grad_c = (sum(part[i] for part in parts) for i in range(2))
    return grad_x, grad_b, grad_c, grad_decay


def solution(mesh):
    placed = (P("ctx", "head"), P("ctx", "head"), P("ctx", None), P("ctx", None), P("head", "ctx"))
    return jax.shard_map(
        shards,
        mesh=mesh,
        in_specs=placed,
        out_specs=(
            P("ctx", "head"),
            P(("ctx", "head"), None),
            P(("ctx", "head"), None),
            P("head", "ctx"),
        ),
        check_vma=False,
    )
```

```python
import functools

import jax
import jax.numpy as jnp
from jax import lax
from jax.experimental import pallas as pl
from jax.experimental.pallas import tpu as pltpu
from jax.sharding import PartitionSpec as P

HEAD_DIM = 64
STATE = 128
HEADS = 8
WIDE = HEADS * HEAD_DIM

F32 = jnp.float32
BF16 = jnp.bfloat16
HIGHEST = lax.Precision.HIGHEST
NN = (((1,), (0,)), ((), ()))
NT = (((1,), (1,)), ((), ()))
TN = (((0,), (0,)), ((), ()))
VMEM_LIMIT = 16 * 1024 * 1024
VMEM_ALL = 61 * 1024 * 1024


def dot(a, b, dims=NN):
    return lax.dot_general(a, b, dims, preferred_element_type=F32)


def dot_full(a, b, dims=NN):
    return lax.dot_general(a, b, dims, precision=HIGHEST, preferred_element_type=F32)


def halves(a):
    high = a.astype(BF16)
    return high, (a - high.astype(F32)).astype(BF16)


def dot_halves(a, b, dims=NN):
    high, low = halves(a)
    return dot(high, b, dims) + dot(low, b, dims)


def at_least(shape, row_dim, col_dim):
    return lax.broadcasted_iota(jnp.int32, shape, row_dim) >= lax.broadcasted_iota(
        jnp.int32, shape, col_dim
    )


def spread_matrix(heads):
    shape = (heads, heads * HEAD_DIM)
    lane = lax.broadcasted_iota(jnp.int32, shape, 1)
    first = lax.broadcasted_iota(jnp.int32, shape, 0) * HEAD_DIM
    return jnp.where((lane >= first) & (lane < first + HEAD_DIM), 1.0, 0.0).astype(F32)


def lower_ones(length, row_dim, col_dim):
    return jnp.where(at_least((length, length), row_dim, col_dim), 1.0, 0.0).astype(F32)


def per_head(values):
    spread = spread_matrix(values.shape[1] // HEAD_DIM).astype(BF16)
    high, low = halves(values)
    return dot(spread, high, NT) + dot(spread, low, NT)


def first_half(rows):
    return lax.broadcasted_iota(jnp.int32, (rows, 2 * HEAD_DIM), 1) < HEAD_DIM


def over_lanes(columns):
    rows, heads = columns.shape
    half = first_half(rows)
    parts = []
    for head in range(0, heads, 2):
        left = jnp.broadcast_to(columns[:, head : head + 1], half.shape)
        right = jnp.broadcast_to(columns[:, head + 1 : head + 2], half.shape)
        parts.append(jnp.where(half, left, right))
    return jnp.concatenate(parts, axis=1)


def local_kernel(groups, decay_in, x_in, dy_in, b_in, c_in, *refs):
    chunks = x_in.shape[1] // WIDE
    late = chunks // 2
    count = 5 + chunks + late
    lower = lax.axis_index("ctx") // 2 < groups // 2
    near_at = pl.multiple_of(jnp.where(lower, 0, STATE), STATE)
    far_at = pl.multiple_of(jnp.where(lower, STATE, 0), STATE)
    outs = refs[:count]
    decay_ref, x_ref, dy_ref, b_ref, c_ref = refs[count : count + 5]
    kept = refs[count + 5 : count + 10]
    rows_ref, columns_ref, into_ref, from_ref, totals_ref = kept
    messages, small_sem, wide_sem, out_sem = refs[count + 10 :]
    pending = []

    def leave(source, target):
        copy = pltpu.make_async_copy(source, target, out_sem.at[len(pending)])
        copy.start()
        pending.append(copy)

    small = [
        pltpu.make_async_copy(source, target, small_sem.at[i])
        for i, (source, target) in enumerate(((decay_in, decay_ref), (b_in, b_ref), (c_in, c_ref)))
    ]
    wide = []
    for chunk in range(chunks):
        lanes = pl.ds(chunk * WIDE, WIDE)
        wide.append(
            [
                pltpu.make_async_copy(source.at[:, lanes], target.at[:, lanes], wide_sem.at[i, chunk])
                for i, (source, target) in enumerate(((x_in, x_ref), (dy_in, dy_ref)))
            ]
        )
    for copy in small + [copy for pair in wide for copy in pair]:
        copy.start()
    small[0].wait()
    length = decay_ref.shape[1]
    rows = dot_full(decay_ref[...], lower_ones(length, 1, 0))
    rows_ref[...] = rows
    columns = rows.T
    into_end = jnp.exp(rows[:, length - 1 : length] - rows)
    from_start = jnp.exp(rows)
    into_column = into_end.T
    from_column = from_start.T
    small[1].wait()
    small[2].wait()
    b_t = b_ref[...].astype(F32).T
    c_t = c_ref[...].astype(F32).T
    half = first_half(STATE)

    def gathered(proj, factors, values_ref, pair):
        head = 2 * pair
        scaled = jnp.concatenate(
            [proj * factors[head : head + 1, :], proj * factors[head + 1 : head + 2, :]], axis=0
        )
        sums = dot(scaled.astype(BF16), values_ref[:, pl.ds(pair * STATE, STATE)])
        return jnp.where(half, sums[:STATE], sums[STATE:])

    for chunk in range(chunks):
        lanes = pl.ds(chunk * WIDE, WIDE)
        heads = slice(chunk * HEADS, (chunk + 1) * HEADS)
        pairs = range(chunk * HEADS // 2, (chunk + 1) * HEADS // 2)
        columns_ref[chunk] = columns[:, heads]
        into_ref[chunk] = into_column[:, heads]
        from_ref[chunk] = from_column[:, heads]
        totals_ref[:, lanes] = over_lanes(from_column[length - 8 :, heads])[7:8, :]
        for place, (proj, factors, values_ref, rows_at) in enumerate(
            ((b_t, into_end, x_ref, near_at), (c_t, from_start, dy_ref, far_at))
        ):
            wide[chunk][place].wait()
            for pair in pairs:
                at = (pair - pairs[0]) * STATE
                messages[chunk, pl.ds(rows_at, STATE), at : at + STATE] = gathered(
                    proj, factors, values_ref, pair
                )
        if chunk < chunks - late:
            leave(messages.at[chunk], outs[5 + chunk])
        else:
            place = 5 + late + 2 * (chunk - late)
            leave(messages.at[chunk, :STATE], outs[place])
            leave(messages.at[chunk, STATE:], outs[place + 1])
    for source, target in zip(kept, outs[:5]):
        leave(source, target)
    for copy in pending:
        copy.wait()


def intra_kernel(
    rows_ref,
    columns_ref,
    into_ref,
    from_ref,
    x_ref,
    dy_ref,
    b_ref,
    c_ref,
    gb_in_ref,
    gc_in_ref,
    dx_ref,
    xs_ref,
    dys_ref,
    change_ref,
    gb_ref,
    gc_ref,
    table_ref,
):
    step = pl.program_id(0)
    rows = rows_ref[...]
    columns = columns_ref[0]
    xs_ref[...] = (x_ref[...].astype(F32) * over_lanes(into_ref[0])).astype(BF16)
    dys_ref[...] = (dy_ref[...].astype(F32) * over_lanes(from_ref[0])).astype(BF16)
    length = rows.shape[1]
    b, c = b_ref[...], c_ref[...]
    scores = dot(b, c, NT)
    size = STATE
    keep = at_least((size, size), 1, 0)
    half = first_half(size)
    blocks = length // size

    @pl.when(step == 0)
    def _():
        table_ref[...] = jnp.zeros_like(table_ref)


    for pair in range(HEADS // 2):
        lanes = slice(pair * 2 * HEAD_DIM, (pair + 1) * 2 * HEAD_DIM)
        dy2 = dy_ref[:, lanes]
        sums = [None, None]
        for block in range(blocks):
            first = block * size
            x2 = x_ref[first : first + size, lanes].astype(F32)
            parts = []
            for side in range(2):
                head = 2 * pair + side
                own = half if side == 0 else jnp.logical_not(half)
                x1 = jnp.where(own, x2, 0.0).astype(BF16)
                pairs = dot(x1, dy2[first:], NT)
                gap = rows[head : head + 1, first:] - columns[first : first + size, head : head + 1]
                near = jnp.where(keep, gap[:, :size], -1e30)
                if length - first > size:
                    near = jnp.concatenate([near, gap[:, size:]], axis=1)
                mask = jnp.exp(near)
                weights = (mask * scores[first : first + size, first:]).astype(BF16)
                table_ref[first : first + size, first:] += mask * pairs
                change = jnp.sum(weights.astype(F32) * pairs, axis=0, keepdims=True)
                if block == 0:
                    sums[side] = change
                else:
                    sums[side] = jnp.concatenate(
                        [sums[side][:, :first], sums[side][:, first:] + change], axis=1
                    )
                parts.append(dot(weights, dy2[first:]))
            dx_ref[first : first + size, lanes] = jnp.where(half, parts[0], parts[1])
        for side in range(2):
            head = 2 * pair + side
            change_ref[head : head + 1, :] = sums[side]

    change_ref[...] -= per_head(x_ref[...].astype(F32) * dx_ref[...])

    @pl.when(step == pl.num_programs(0) - 1)
    def _():
        table = table_ref[...]
        gb_ref[...] = gb_in_ref[...] + dot_halves(table, c)
        gc_ref[...] = gc_in_ref[...] + dot_halves(table, b, TN)


def inter_kernel(
    chunk,
    into_ref,
    state_in_ref,
    adjoint_in_ref,
    total_ref,
    xs_ref,
    dys_ref,
    b_ref,
    c_ref,
    dx_ref,
    gb_ref,
    gc_ref,
    gx_ref,
    change_ref,
    earlier_ref,
    later_ref,
    gb_out_ref,
    gc_out_ref,
):
    lanes = slice(chunk * WIDE, (chunk + 1) * WIDE)
    state_in = state_in_ref[...]
    adjoint_in = adjoint_in_ref[...]
    state_low = state_in.astype(BF16)
    adjoint_low = adjoint_in.astype(BF16)
    xs = xs_ref[...]
    dys = dys_ref[...]
    gb_out_ref[...] = gb_ref[...] + dot(xs, adjoint_low, NT)
    gc_out_ref[...] = gc_ref[...] + dot(dys, state_low, NT)
    outer = dot(b_ref[...], adjoint_low)
    gx_ref[...] = (dx_ref[...] + over_lanes(into_ref[chunk]) * outer).astype(BF16)
    change_ref[...] = per_head(dys.astype(F32) * dot(c_ref[...], state_low))
    earlier_ref[...] = per_head(xs.astype(F32) * outer)
    later_ref[...] = per_head(total_ref[:, lanes] * state_in * adjoint_in)


def suffix_kernel(chunks, *refs):
    out_ref = refs[-1]
    length = out_ref.shape[1]

    def joined(place):
        return jnp.concatenate([ref[...] for ref in refs[place * chunks : (place + 1) * chunks]], 0)

    from_here = dot_full(joined(0) + joined(1), lower_ones(length, 0, 1))
    before = dot_full(joined(2), 1.0 - lower_ones(length, 0, 1))
    out_ref[...] = from_here + before + jnp.sum(joined(3), axis=1, keepdims=True)


def params(limit=VMEM_LIMIT):
    return pltpu.CompilerParams(vmem_limit_bytes=limit)


def cost(flops, nbytes):
    return pl.CostEstimate(flops=flops, bytes_accessed=nbytes, transcendentals=0)


def shape(dims, dtype=F32):
    return jax.ShapeDtypeStruct(dims, dtype)


def vmem(count):
    return [pl.BlockSpec(memory_space=pltpu.VMEM)] * count


def local_states(groups, log_decay, x, dy, b, c):
    tokens, width = x.shape
    heads = log_decay.shape[0]
    chunks = width // WIDE
    kept = [(heads, tokens)] + [(chunks, tokens, HEADS)] * 3 + [(1, width)]
    late = chunks // 2
    outs = kept + [(2 * STATE, WIDE)] * (chunks - late) + [(STATE, WIDE)] * (2 * late)
    hbm = pl.BlockSpec(memory_space=pltpu.HBM)
    outs = pl.pallas_call(
        functools.partial(local_kernel, groups),
        in_specs=[hbm] * 5,
        out_specs=[hbm] * len(outs),
        out_shape=[shape(dims) for dims in outs],
        scratch_shapes=[
            pltpu.VMEM(log_decay.shape, F32),
            pltpu.VMEM(x.shape, BF16),
            pltpu.VMEM(x.shape, BF16),
            pltpu.VMEM(b.shape, BF16),
            pltpu.VMEM(b.shape, BF16),
            *[pltpu.VMEM(dims, F32) for dims in kept],
            pltpu.VMEM((chunks, 2 * STATE, WIDE), F32),
            pltpu.SemaphoreType.DMA((3,)),
            pltpu.SemaphoreType.DMA((2, chunks)),
            pltpu.SemaphoreType.DMA((len(outs),)),
        ],
        compiler_params=params(VMEM_ALL),
        cost_estimate=cost(4 * tokens * STATE * width, 12 * tokens * width),
        name="local_states",
    )(log_decay, x, dy, b, c)
    pairs, sides = outs[5 : 5 + chunks - late], outs[5 + chunks - late :]
    return outs[:5], pairs, [sides[i : i + 2] for i in range(0, 2 * late, 2)]


def intra(chunk, rows, columns, into, start, x, dy, b, c, gb, gc):
    tokens = x.shape[0]
    wide = pl.BlockSpec((tokens, WIDE), lambda k: (0, chunk))
    own = pl.BlockSpec((tokens, WIDE), lambda k: (0, 0))
    proj = pl.BlockSpec((tokens, STATE), lambda k: (0, 0))
    return pl.pallas_call(
        intra_kernel,
        grid=(1,),
        in_specs=[
            pl.BlockSpec((HEADS, tokens), lambda k: (chunk, 0)),
            *[pl.BlockSpec((1, tokens, HEADS), lambda k: (chunk, 0, 0))] * 3,
            wide,
            wide,
            *[proj] * 4,
        ],
        out_specs=[own, own, own, pl.BlockSpec((HEADS, tokens), lambda k: (0, 0)), proj, proj],
        out_shape=[
            shape((tokens, WIDE)),
            shape((tokens, WIDE), BF16),
            shape((tokens, WIDE), BF16),
            shape((HEADS, tokens)),
            shape((tokens, STATE)),
            shape((tokens, STATE)),
        ],
        scratch_shapes=[pltpu.VMEM((tokens, tokens), F32)],
        compiler_params=params(),
        cost_estimate=cost(4 * tokens * tokens * WIDE, 8 * tokens * WIDE),
        name="intra",
    )(rows, columns, into, start, x, dy, b, c, gb, gc)


def inter(chunk, into, state_in, adjoint_in, totals, xs, dys, b, c, dx, gb, gc):
    tokens = xs.shape[0]
    args = (into, state_in, adjoint_in, totals, xs, dys, b, c, dx, gb, gc)
    out_shape = [
        shape((tokens, WIDE), BF16),
        shape((HEADS, tokens)),
        shape((HEADS, tokens)),
        shape((HEADS, STATE)),
        shape((tokens, STATE)),
        shape((tokens, STATE)),
    ]
    return pl.pallas_call(
        functools.partial(inter_kernel, chunk),
        in_specs=vmem(len(args)),
        out_specs=vmem(len(out_shape)),
        out_shape=out_shape,
        compiler_params=params(),
        cost_estimate=cost(8 * tokens * STATE * WIDE, 16 * tokens * WIDE),
        name="inter",
    )(*args)


def suffix_sums(*parts):
    chunks = len(parts[0])
    args = [item for part in parts for item in part]
    return pl.pallas_call(
        functools.partial(suffix_kernel, chunks),
        in_specs=vmem(len(args)),
        out_specs=vmem(1)[0],
        out_shape=shape((chunks * HEADS, args[0].shape[1])),
        compiler_params=params(),
        cost_estimate=cost(0, 1 << 17),
        name="suffix_sums",
    )(*args)


class Chunk:
    def __init__(self, first, message, own, other, diagonal, second):
        self.first, self.own, self.other, self.second = first, own, other, second
        self.state, self.adjoint = message[:STATE], message[STATE:]
        both = own * other
        if first:
            self.step_f = self.step_b = both
            self.seen_f = self.seen_b = jnp.ones_like(own)
        else:
            self.forward, self.backward = self.state, self.adjoint
            self.step_f, self.step_b = jnp.where(second, both, own), jnp.where(second, own, both)
            self.seen_f = jnp.where(second, 1.0, diagonal)
            self.seen_b = jnp.where(second, diagonal, 1.0)

    def joined(self, got):
        self.got_f, self.got_b = got[:STATE], got[STATE:]
        own, other = self.own, self.other
        self.forward = jnp.where(
            self.second, own * self.got_f + self.state, other * self.state + self.got_f
        )
        self.backward = jnp.where(
            self.second, self.got_b + other * self.adjoint, self.adjoint + own * self.got_b
        )

    def leaving_f(self, carried):
        return self.step_f * carried + self.forward

    def leaving_b(self, carried):
        return self.step_b * carried + self.backward

    def message(self):
        send_f = jnp.where(self.second, self.in_f, self.own * self.in_f + self.state)
        send_b = jnp.where(self.second, self.own * self.in_b + self.adjoint, self.in_b)
        return jnp.concatenate([send_f, send_b], axis=0)

    def entering(self, got=None):
        decayed_f = jnp.where(self.second, self.other, 1.0) * self.in_f
        decayed_b = jnp.where(self.second, 1.0, self.other) * self.in_b
        if got is not None:
            return decayed_f + got[:STATE], decayed_b + got[STATE:]
        return (
            decayed_f + jnp.where(self.second, self.got_f, 0.0),
            decayed_b + jnp.where(self.second, 0.0, self.got_b),
        )


def between(links):
    return [(2 * s + side, 2 * t + side) for s, t in links for side in range(2)]


def group_scan(chunk, group, groups):
    carried_f, carried_b = jnp.zeros_like(chunk.forward), jnp.zeros_like(chunk.backward)
    for hop in range(1, groups):
        send = jnp.where(
            group == groups - hop, chunk.leaving_b(carried_b), chunk.leaving_f(carried_f)
        )
        links = [(hop - 1, hop), (groups - hop, groups - hop - 1)]
        got = lax.ppermute(send, "ctx", between(links))
        carried_f = jnp.where(group == hop, chunk.seen_f * got, carried_f)
        carried_b = jnp.where(group == groups - hop - 1, chunk.seen_b * got, carried_b)
    chunk.in_f, chunk.in_b = carried_f, carried_b


def fence(*items):
    return lax.optimization_barrier(items)


def shards(inputs, grad_out, b_proj, c_proj, log_decay):
    count = lax.axis_size("ctx")
    mine = lax.axis_index("ctx")
    second = mine % 2 == 1
    group, groups = mine // 2, count // 2

    def permute(value, links):
        return lax.ppermute(value, "ctx", links)

    swap = [(i, i ^ 1) for i in range(count)]
    diagonals = [(2 * g + 1, 2 * g + 2) for g in range(groups - 1)]
    diagonals += [(t, s) for s, t in diagonals]
    lower = group < groups // 2
    inner = (group > 0) & (group < groups - 1)

    (rows, columns, into, start, totals), pairs, sides = local_states(
        groups, log_decay, inputs, grad_out, b_proj, c_proj
    )
    late = len(pairs)
    chunks = late + len(sides)
    own = totals
    other = permute(own, swap)
    diagonal = permute(own, diagonals)
    none = jnp.zeros((inputs.shape[0], STATE), F32)
    near = [None] * chunks

    def local(k, rows, gb, gc):
        *near[k], gb, gc = intra(
            k, rows, columns, into, start, inputs, grad_out, b_proj, c_proj, gb, gc
        )
        return gb, gc

    def carried(k, entering, gb, gc):
        dx, xs, dys, _ = near[k]
        return inter(k, into, *entering, totals, xs, dys, b_proj, c_proj, dx, gb, gc)

    def ways(forward, backward):
        return jnp.where(lower, forward, backward), jnp.where(lower, backward, forward)

    far = [None] * chunks
    if groups == 4 and chunks == 4:
        middle = between([(1, 2), (2, 1)])
        steps = between([(0, 1), (1, 0), (2, 3), (3, 2)])
        (near2, far2), (near3, far3) = sides

        pair0 = permute(pairs[0], swap)
        hop2 = permute(near2, steps)
        message1 = pairs[1]
        pair1 = permute(fence(message1, other)[0], swap)

        def after(value, *events):
            return fence(value, *events)[0]


        one, zero = jnp.ones_like(own), jnp.zeros_like(own)
        both = own * other
        mine_n, mine_f = ways(jnp.where(second, one, other), jnp.where(second, other, one))
        theirs_n, theirs_f = ways(jnp.where(second, own, one), jnp.where(second, one, own))
        seen_n, seen_f = ways(
            jnp.where(second, one, diagonal), jnp.where(second, diagonal, one)
        )
        step_n, step_f = ways(jnp.where(second, both, own), jnp.where(second, own, both))
        pass_n, pass_f = step_n * seen_n, step_f * seen_f
        cross_n, cross_f = ways(jnp.where(second, one, own), jnp.where(second, own, one))
        cross_n = jnp.where(inner, cross_n * seen_n, zero)
        cross_f = cross_f * seen_f
        with_n, with_f = ways(jnp.where(second, zero, one), jnp.where(second, one, zero))
        last_n, last_f = ways(jnp.where(second, other, one), jnp.where(second, one, other))
        mate_n, mate_f = ways(jnp.where(second, one, zero), jnp.where(second, zero, one))
        reach_n = jnp.where(inner, last_n, zero)

        def at(row, k):
            return row[:, k * WIDE : (k + 1) * WIDE]

        mid2 = permute(at(pass_n, 2) * hop2 + near2, middle)
        hop3 = permute(after(near3, hop2), steps)
        gb, gc = local(0, after(rows, hop2), none, none)

        sum0 = at(mine_n, 0) * pairs[0][:STATE] + at(theirs_n, 0) * pair0[:STATE]
        side2 = permute(jnp.where(inner, at(pass_f, 2) * mid2 + far2, sum0), steps)
        mid3 = permute(at(pass_n, 3) * hop3 + near3, middle)
        cross2 = permute(at(cross_n, 2) * hop2 + at(with_n, 2) * near2, swap)
        gb, gc = local(1, after(rows, mid2), gb, gc)

        sum1 = at(mine_n, 1) * message1[:STATE] + at(theirs_n, 1) * pair1[:STATE]
        side3 = permute(jnp.where(inner, at(pass_f, 3) * mid3 + far3, sum1), steps)
        mid0 = permute(at(both, 0) * side2 + sum0, middle)
        end2 = at(cross_f, 2) * jnp.where(inner, mid2, side2) + at(with_f, 2) * far2
        cross2f = permute(end2, swap)
        cross3 = permute(at(cross_n, 3) * hop3 + at(with_n, 3) * near3, swap)
        gb, gc = local(2, after(rows, side2), gb, gc)

        rest0 = at(mine_f, 0) * pairs[0][STATE:] + at(theirs_f, 0) * pair0[STATE:]
        last0 = permute(at(both, 0) * mid0 + rest0, steps)
        mid1 = permute(at(both, 1) * side3 + sum1, middle)
        end3 = at(cross_f, 3) * jnp.where(inner, mid3, side3) + at(with_f, 3) * far3
        cross3f = permute(end3, swap)
        gb, gc = local(3, after(rows, side3), gb, gc)

        rest1 = at(mine_f, 1) * message1[STATE:] + at(theirs_f, 1) * pair1[STATE:]
        last1 = permute(at(both, 1) * mid1 + rest1, steps)

        def entering(k, first, near, middle, far, got_near, got_far):
            far = jnp.where(inner, middle, far)
            if first:
                near = at(reach_n, k) * near + at(mate_n, k) * got_near
                far = at(last_f, k) * far + at(mate_f, k) * got_far
            else:
                near = at(reach_n * seen_n, k) * near + got_near
                far = at(last_f * seen_f, k) * far + got_far
            return ways(near, far)

        enter0 = entering(0, True, side2, mid0, last0, pair0[:STATE], pair0[STATE:])
        *far[0], gb, gc = carried(0, enter0, gb, gc)
        enter2 = entering(2, False, hop2, mid2, side2, cross2, cross2f)
        *far[2], gb, gc = carried(2, enter2, gb, gc)
        cross3f, gb, gc = fence(cross3f, gb, gc)
        enter3 = entering(3, False, hop3, mid3, side3, cross3, cross3f)
        *far[3], gb, gc = carried(3, enter3, gb, gc)
        last1, gb, gc = fence(last1, gb, gc)
        enter1 = entering(1, True, side3, mid1, last1, pair1[:STATE], pair1[STATE:])
        *far[1], gb, gc = carried(1, enter1, gb, gc)
    else:
        gb = gc = none
        for k in range(chunks):
            gb, gc = local(k, rows, gb, gc)
            first = k < late
            lanes = slice(k * WIDE, (k + 1) * WIDE)
            message = pairs[k] if first else jnp.concatenate(sides[k - late], axis=0)
            flipped = jnp.concatenate([message[STATE:], message[:STATE]], axis=0)
            message = jnp.where(lower, message, flipped)
            chunk = Chunk(
                first, message, own[:, lanes], other[:, lanes], diagonal[:, lanes], second
            )
            if first:
                chunk.joined(permute(message, swap))
            group_scan(chunk, group, groups)
            got = None if first else permute(chunk.message(), swap)
            *far[k], gb, gc = carried(k, chunk.entering(got), gb, gc)
    grad_x = jnp.concatenate([item[0] for item in far], axis=1)
    grad_decay = suffix_sums([item[3] for item in near], *([item[i] for item in far] for i in (1, 2, 3)))

    ranks = lax.axis_size("head")
    rank = lax.axis_index("head")
    size = gb.shape[0] // ranks
    sums = jnp.stack([gb, gc])

    def piece(owner):
        return lax.dynamic_slice_in_dim(sums, owner * size, size, axis=1)

    parts = [piece(rank)]
    for step in range(1, ranks):
        links = [(i, i ^ step) for i in range(ranks)]
        parts.append(lax.ppermute(piece(rank ^ step), "head", links))
    grad_b, grad_c = (sum(part[i] for part in parts) for i in range(2))
    return grad_x, grad_b, grad_c, grad_decay


def solution(mesh):
    placed = (P("ctx", "head"), P("ctx", "head"), P("ctx", None), P("ctx", None), P("head", "ctx"))
    return jax.shard_map(
        shards,
        mesh=mesh,
        in_specs=placed,
        out_specs=(
            P("ctx", "head"),
            P(("ctx", "head"), None),
            P(("ctx", "head"), None),
            P("head", "ctx"),
        ),
        check_vma=False,
    )
```

```python
import functools

import jax
import jax.numpy as jnp
from jax import lax
from jax.experimental import pallas as pl
from jax.experimental.pallas import tpu as pltpu
from jax.sharding import PartitionSpec as P

HEAD_DIM = 64
STATE = 128
HEADS = 8
WIDE = HEADS * HEAD_DIM

F32 = jnp.float32
BF16 = jnp.bfloat16
HIGHEST = lax.Precision.HIGHEST
NN = (((1,), (0,)), ((), ()))
NT = (((1,), (1,)), ((), ()))
TN = (((0,), (0,)), ((), ()))
VMEM_LIMIT = 16 * 1024 * 1024
VMEM_ALL = 61 * 1024 * 1024


def dot(a, b, dims=NN):
    return lax.dot_general(a, b, dims, preferred_element_type=F32)


def dot_full(a, b, dims=NN):
    return lax.dot_general(a, b, dims, precision=HIGHEST, preferred_element_type=F32)


def halves(a):
    high = a.astype(BF16)
    return high, (a - high.astype(F32)).astype(BF16)


def dot_halves(a, b, dims=NN):
    high, low = halves(a)
    return dot(high, b, dims) + dot(low, b, dims)


def at_least(shape, row_dim, col_dim):
    return lax.broadcasted_iota(jnp.int32, shape, row_dim) >= lax.broadcasted_iota(
        jnp.int32, shape, col_dim
    )


def spread_matrix(heads):
    shape = (heads, heads * HEAD_DIM)
    lane = lax.broadcasted_iota(jnp.int32, shape, 1)
    first = lax.broadcasted_iota(jnp.int32, shape, 0) * HEAD_DIM
    return jnp.where((lane >= first) & (lane < first + HEAD_DIM), 1.0, 0.0).astype(F32)


def lower_ones(length, row_dim, col_dim):
    return jnp.where(at_least((length, length), row_dim, col_dim), 1.0, 0.0).astype(F32)


def per_head(values):
    spread = spread_matrix(values.shape[1] // HEAD_DIM).astype(BF16)
    high, low = halves(values)
    return dot(spread, high, NT) + dot(spread, low, NT)


def first_half(rows):
    return lax.broadcasted_iota(jnp.int32, (rows, 2 * HEAD_DIM), 1) < HEAD_DIM


def over_lanes(columns):
    rows, heads = columns.shape
    half = first_half(rows)
    parts = []
    for head in range(0, heads, 2):
        left = jnp.broadcast_to(columns[:, head : head + 1], half.shape)
        right = jnp.broadcast_to(columns[:, head + 1 : head + 2], half.shape)
        parts.append(jnp.where(half, left, right))
    return jnp.concatenate(parts, axis=1)


def local_kernel(groups, decay_in, x_in, dy_in, b_in, c_in, *refs):
    chunks = x_in.shape[1] // WIDE
    late = chunks // 2
    count = 5 + chunks + late
    lower = lax.axis_index("ctx") // 2 < groups // 2
    near_at = pl.multiple_of(jnp.where(lower, 0, STATE), STATE)
    far_at = pl.multiple_of(jnp.where(lower, STATE, 0), STATE)
    outs = refs[:count]
    decay_ref, x_ref, dy_ref, b_ref, c_ref = refs[count : count + 5]
    kept = refs[count + 5 : count + 10]
    rows_ref, columns_ref, into_ref, from_ref, totals_ref = kept
    messages, small_sem, wide_sem, out_sem = refs[count + 10 :]
    pending = []

    def leave(source, target):
        copy = pltpu.make_async_copy(source, target, out_sem.at[len(pending)])
        copy.start()
        pending.append(copy)

    small = [
        pltpu.make_async_copy(source, target, small_sem.at[i])
        for i, (source, target) in enumerate(((decay_in, decay_ref), (b_in, b_ref), (c_in, c_ref)))
    ]
    wide = []
    for chunk in range(chunks):
        lanes = pl.ds(chunk * WIDE, WIDE)
        wide.append(
            [
                pltpu.make_async_copy(source.at[:, lanes], target.at[:, lanes], wide_sem.at[i, chunk])
                for i, (source, target) in enumerate(((x_in, x_ref), (dy_in, dy_ref)))
            ]
        )
    for copy in small + [copy for pair in wide for copy in pair]:
        copy.start()
    small[0].wait()
    length = decay_ref.shape[1]
    rows = dot_full(decay_ref[...], lower_ones(length, 1, 0))
    rows_ref[...] = rows
    columns = rows.T
    into_end = jnp.exp(rows[:, length - 1 : length] - rows)
    from_start = jnp.exp(rows)
    into_column = into_end.T
    from_column = from_start.T
    for chunk in range(chunks):
        heads = slice(chunk * HEADS, (chunk + 1) * HEADS)
        columns_ref[chunk] = columns[:, heads]
        into_ref[chunk] = into_column[:, heads]
        from_ref[chunk] = from_column[:, heads]
    for source, target in zip(kept[:4], outs[:4]):
        leave(source, target)
    small[1].wait()
    small[2].wait()
    b_t = b_ref[...].astype(F32).T
    c_t = c_ref[...].astype(F32).T
    half = first_half(STATE)

    def gathered(proj, factors, values_ref, pair):
        head = 2 * pair
        scaled = jnp.concatenate(
            [proj * factors[head : head + 1, :], proj * factors[head + 1 : head + 2, :]], axis=0
        )
        sums = dot(scaled.astype(BF16), values_ref[:, pl.ds(pair * STATE, STATE)])
        return jnp.where(half, sums[:STATE], sums[STATE:])

    for chunk in range(chunks):
        lanes = pl.ds(chunk * WIDE, WIDE)
        heads = slice(chunk * HEADS, (chunk + 1) * HEADS)
        pairs = range(chunk * HEADS // 2, (chunk + 1) * HEADS // 2)
        totals_ref[:, lanes] = over_lanes(from_column[length - 8 :, heads])[7:8, :]
        for place, (proj, factors, values_ref, rows_at) in enumerate(
            ((b_t, into_end, x_ref, near_at), (c_t, from_start, dy_ref, far_at))
        ):
            wide[chunk][place].wait()
            for pair in pairs:
                at = (pair - pairs[0]) * STATE
                messages[chunk, pl.ds(rows_at, STATE), at : at + STATE] = gathered(
                    proj, factors, values_ref, pair
                )
        if chunk < chunks - late:
            leave(messages.at[chunk], outs[5 + chunk])
        else:
            place = 5 + late + 2 * (chunk - late)
            leave(messages.at[chunk, :STATE], outs[place])
            leave(messages.at[chunk, STATE:], outs[place + 1])
    leave(totals_ref, outs[4])
    for copy in pending:
        copy.wait()


def intra_kernel(
    rows_ref,
    columns_ref,
    into_ref,
    from_ref,
    x_ref,
    dy_ref,
    b_ref,
    c_ref,
    gb_in_ref,
    gc_in_ref,
    dx_ref,
    xs_ref,
    dys_ref,
    change_ref,
    gb_ref,
    gc_ref,
    table_ref,
):
    step = pl.program_id(0)
    rows = rows_ref[...]
    columns = columns_ref[0]
    xs_ref[...] = (x_ref[...].astype(F32) * over_lanes(into_ref[0])).astype(BF16)
    dys_ref[...] = (dy_ref[...].astype(F32) * over_lanes(from_ref[0])).astype(BF16)
    length = rows.shape[1]
    b, c = b_ref[...], c_ref[...]
    scores = dot(b, c, NT)
    size = STATE
    keep = at_least((size, size), 1, 0)
    half = first_half(size)
    blocks = length // size

    @pl.when(step == 0)
    def _():
        table_ref[...] = jnp.zeros_like(table_ref)


    for pair in range(HEADS // 2):
        lanes = slice(pair * 2 * HEAD_DIM, (pair + 1) * 2 * HEAD_DIM)
        dy2 = dy_ref[:, lanes]
        sums = [None, None]
        for block in range(blocks):
            first = block * size
            x2 = x_ref[first : first + size, lanes].astype(F32)
            parts = []
            for side in range(2):
                head = 2 * pair + side
                own = half if side == 0 else jnp.logical_not(half)
                x1 = jnp.where(own, x2, 0.0).astype(BF16)
                pairs = dot(x1, dy2[first:], NT)
                gap = rows[head : head + 1, first:] - columns[first : first + size, head : head + 1]
                near = jnp.where(keep, gap[:, :size], -1e30)
                if length - first > size:
                    near = jnp.concatenate([near, gap[:, size:]], axis=1)
                mask = jnp.exp(near)
                weights = (mask * scores[first : first + size, first:]).astype(BF16)
                table_ref[first : first + size, first:] += mask * pairs
                change = jnp.sum(weights.astype(F32) * pairs, axis=0, keepdims=True)
                if block == 0:
                    sums[side] = change
                else:
                    sums[side] = jnp.concatenate(
                        [sums[side][:, :first], sums[side][:, first:] + change], axis=1
                    )
                parts.append(dot(weights, dy2[first:]))
            dx_ref[first : first + size, lanes] = jnp.where(half, parts[0], parts[1])
        for side in range(2):
            head = 2 * pair + side
            change_ref[head : head + 1, :] = sums[side]

    change_ref[...] -= per_head(x_ref[...].astype(F32) * dx_ref[...])

    @pl.when(step == pl.num_programs(0) - 1)
    def _():
        table = table_ref[...]
        gb_ref[...] = gb_in_ref[...] + dot_halves(table, c)
        gc_ref[...] = gc_in_ref[...] + dot_halves(table, b, TN)


def inter_kernel(
    chunk,
    into_ref,
    state_in_ref,
    adjoint_in_ref,
    total_ref,
    xs_ref,
    dys_ref,
    b_ref,
    c_ref,
    dx_ref,
    gb_ref,
    gc_ref,
    gx_ref,
    change_ref,
    earlier_ref,
    later_ref,
    gb_out_ref,
    gc_out_ref,
):
    lanes = slice(chunk * WIDE, (chunk + 1) * WIDE)
    state_in = state_in_ref[...]
    adjoint_in = adjoint_in_ref[...]
    state_low = state_in.astype(BF16)
    adjoint_low = adjoint_in.astype(BF16)
    xs = xs_ref[...]
    dys = dys_ref[...]
    gb_out_ref[...] = gb_ref[...] + dot(xs, adjoint_low, NT)
    gc_out_ref[...] = gc_ref[...] + dot(dys, state_low, NT)
    outer = dot(b_ref[...], adjoint_low)
    gx_ref[...] = (dx_ref[...] + over_lanes(into_ref[chunk]) * outer).astype(BF16)
    change_ref[...] = per_head(dys.astype(F32) * dot(c_ref[...], state_low))
    earlier_ref[...] = per_head(xs.astype(F32) * outer)
    later_ref[...] = per_head(total_ref[:, lanes] * state_in * adjoint_in)


def suffix_kernel(chunks, *refs):
    out_ref = refs[-1]
    length = out_ref.shape[1]

    def joined(place):
        return jnp.concatenate([ref[...] for ref in refs[place * chunks : (place + 1) * chunks]], 0)

    from_here = dot_full(joined(0) + joined(1), lower_ones(length, 0, 1))
    before = dot_full(joined(2), 1.0 - lower_ones(length, 0, 1))
    out_ref[...] = from_here + before + jnp.sum(joined(3), axis=1, keepdims=True)


def params(limit=VMEM_LIMIT):
    return pltpu.CompilerParams(vmem_limit_bytes=limit)


def cost(flops, nbytes):
    return pl.CostEstimate(flops=flops, bytes_accessed=nbytes, transcendentals=0)


def shape(dims, dtype=F32):
    return jax.ShapeDtypeStruct(dims, dtype)


def vmem(count):
    return [pl.BlockSpec(memory_space=pltpu.VMEM)] * count


def local_states(groups, log_decay, x, dy, b, c):
    tokens, width = x.shape
    heads = log_decay.shape[0]
    chunks = width // WIDE
    kept = [(heads, tokens)] + [(chunks, tokens, HEADS)] * 3 + [(1, width)]
    late = chunks // 2
    outs = kept + [(2 * STATE, WIDE)] * (chunks - late) + [(STATE, WIDE)] * (2 * late)
    hbm = pl.BlockSpec(memory_space=pltpu.HBM)
    outs = pl.pallas_call(
        functools.partial(local_kernel, groups),
        in_specs=[hbm] * 5,
        out_specs=[hbm] * len(outs),
        out_shape=[shape(dims) for dims in outs],
        scratch_shapes=[
            pltpu.VMEM(log_decay.shape, F32),
            pltpu.VMEM(x.shape, BF16),
            pltpu.VMEM(x.shape, BF16),
            pltpu.VMEM(b.shape, BF16),
            pltpu.VMEM(b.shape, BF16),
            *[pltpu.VMEM(dims, F32) for dims in kept],
            pltpu.VMEM((chunks, 2 * STATE, WIDE), F32),
            pltpu.SemaphoreType.DMA((3,)),
            pltpu.SemaphoreType.DMA((2, chunks)),
            pltpu.SemaphoreType.DMA((len(outs),)),
        ],
        compiler_params=params(VMEM_ALL),
        cost_estimate=cost(4 * tokens * STATE * width, 12 * tokens * width),
        name="local_states",
    )(log_decay, x, dy, b, c)
    pairs, sides = outs[5 : 5 + chunks - late], outs[5 + chunks - late :]
    return outs[:5], pairs, [sides[i : i + 2] for i in range(0, 2 * late, 2)]


def intra(chunk, rows, columns, into, start, x, dy, b, c, gb, gc):
    tokens = x.shape[0]
    wide = pl.BlockSpec((tokens, WIDE), lambda k: (0, chunk))
    own = pl.BlockSpec((tokens, WIDE), lambda k: (0, 0))
    proj = pl.BlockSpec((tokens, STATE), lambda k: (0, 0))
    return pl.pallas_call(
        intra_kernel,
        grid=(1,),
        in_specs=[
            pl.BlockSpec((HEADS, tokens), lambda k: (chunk, 0)),
            *[pl.BlockSpec((1, tokens, HEADS), lambda k: (chunk, 0, 0))] * 3,
            wide,
            wide,
            *[proj] * 4,
        ],
        out_specs=[own, own, own, pl.BlockSpec((HEADS, tokens), lambda k: (0, 0)), proj, proj],
        out_shape=[
            shape((tokens, WIDE)),
            shape((tokens, WIDE), BF16),
            shape((tokens, WIDE), BF16),
            shape((HEADS, tokens)),
            shape((tokens, STATE)),
            shape((tokens, STATE)),
        ],
        scratch_shapes=[pltpu.VMEM((tokens, tokens), F32)],
        compiler_params=params(),
        cost_estimate=cost(4 * tokens * tokens * WIDE, 8 * tokens * WIDE),
        name="intra",
    )(rows, columns, into, start, x, dy, b, c, gb, gc)


def inter(chunk, into, state_in, adjoint_in, totals, xs, dys, b, c, dx, gb, gc):
    tokens = xs.shape[0]
    args = (into, state_in, adjoint_in, totals, xs, dys, b, c, dx, gb, gc)
    out_shape = [
        shape((tokens, WIDE), BF16),
        shape((HEADS, tokens)),
        shape((HEADS, tokens)),
        shape((HEADS, STATE)),
        shape((tokens, STATE)),
        shape((tokens, STATE)),
    ]
    return pl.pallas_call(
        functools.partial(inter_kernel, chunk),
        in_specs=vmem(len(args)),
        out_specs=vmem(len(out_shape)),
        out_shape=out_shape,
        compiler_params=params(),
        cost_estimate=cost(8 * tokens * STATE * WIDE, 16 * tokens * WIDE),
        name="inter",
    )(*args)


def suffix_sums(*parts):
    chunks = len(parts[0])
    args = [item for part in parts for item in part]
    return pl.pallas_call(
        functools.partial(suffix_kernel, chunks),
        in_specs=vmem(len(args)),
        out_specs=vmem(1)[0],
        out_shape=shape((chunks * HEADS, args[0].shape[1])),
        compiler_params=params(),
        cost_estimate=cost(0, 1 << 17),
        name="suffix_sums",
    )(*args)


class Chunk:
    def __init__(self, first, message, own, other, diagonal, second):
        self.first, self.own, self.other, self.second = first, own, other, second
        self.state, self.adjoint = message[:STATE], message[STATE:]
        both = own * other
        if first:
            self.step_f = self.step_b = both
            self.seen_f = self.seen_b = jnp.ones_like(own)
        else:
            self.forward, self.backward = self.state, self.adjoint
            self.step_f, self.step_b = jnp.where(second, both, own), jnp.where(second, own, both)
            self.seen_f = jnp.where(second, 1.0, diagonal)
            self.seen_b = jnp.where(second, diagonal, 1.0)

    def joined(self, got):
        self.got_f, self.got_b = got[:STATE], got[STATE:]
        own, other = self.own, self.other
        self.forward = jnp.where(
            self.second, own * self.got_f + self.state, other * self.state + self.got_f
        )
        self.backward = jnp.where(
            self.second, self.got_b + other * self.adjoint, self.adjoint + own * self.got_b
        )

    def leaving_f(self, carried):
        return self.step_f * carried + self.forward

    def leaving_b(self, carried):
        return self.step_b * carried + self.backward

    def message(self):
        send_f = jnp.where(self.second, self.in_f, self.own * self.in_f + self.state)
        send_b = jnp.where(self.second, self.own * self.in_b + self.adjoint, self.in_b)
        return jnp.concatenate([send_f, send_b], axis=0)

    def entering(self, got=None):
        decayed_f = jnp.where(self.second, self.other, 1.0) * self.in_f
        decayed_b = jnp.where(self.second, 1.0, self.other) * self.in_b
        if got is not None:
            return decayed_f + got[:STATE], decayed_b + got[STATE:]
        return (
            decayed_f + jnp.where(self.second, self.got_f, 0.0),
            decayed_b + jnp.where(self.second, 0.0, self.got_b),
        )


def between(links):
    return [(2 * s + side, 2 * t + side) for s, t in links for side in range(2)]


def group_scan(chunk, group, groups):
    carried_f, carried_b = jnp.zeros_like(chunk.forward), jnp.zeros_like(chunk.backward)
    for hop in range(1, groups):
        send = jnp.where(
            group == groups - hop, chunk.leaving_b(carried_b), chunk.leaving_f(carried_f)
        )
        links = [(hop - 1, hop), (groups - hop, groups - hop - 1)]
        got = lax.ppermute(send, "ctx", between(links))
        carried_f = jnp.where(group == hop, chunk.seen_f * got, carried_f)
        carried_b = jnp.where(group == groups - hop - 1, chunk.seen_b * got, carried_b)
    chunk.in_f, chunk.in_b = carried_f, carried_b


def fence(*items):
    return lax.optimization_barrier(items)


def shards(inputs, grad_out, b_proj, c_proj, log_decay):
    count = lax.axis_size("ctx")
    mine = lax.axis_index("ctx")
    second = mine % 2 == 1
    group, groups = mine // 2, count // 2

    def permute(value, links):
        return lax.ppermute(value, "ctx", links)

    swap = [(i, i ^ 1) for i in range(count)]
    diagonals = [(2 * g + 1, 2 * g + 2) for g in range(groups - 1)]
    diagonals += [(t, s) for s, t in diagonals]
    lower = group < groups // 2
    inner = (group > 0) & (group < groups - 1)

    (rows, columns, into, start, totals), pairs, sides = local_states(
        groups, log_decay, inputs, grad_out, b_proj, c_proj
    )
    late = len(pairs)
    chunks = late + len(sides)
    own = totals
    other = permute(own, swap)
    diagonal = permute(own, diagonals)
    none = jnp.zeros((inputs.shape[0], STATE), F32)
    near = [None] * chunks

    def local(k, rows, gb, gc):
        *near[k], gb, gc = intra(
            k, rows, columns, into, start, inputs, grad_out, b_proj, c_proj, gb, gc
        )
        return gb, gc

    def carried(k, entering, gb, gc):
        dx, xs, dys, _ = near[k]
        return inter(k, into, *entering, totals, xs, dys, b_proj, c_proj, dx, gb, gc)

    def ways(forward, backward):
        return jnp.where(lower, forward, backward), jnp.where(lower, backward, forward)

    far = [None] * chunks
    if groups == 4 and chunks == 4:
        middle = between([(1, 2), (2, 1)])
        steps = between([(0, 1), (1, 0), (2, 3), (3, 2)])
        (near2, far2), (near3, far3) = sides

        pair0 = permute(pairs[0], swap)
        hop2 = permute(near2, steps)
        message1 = pairs[1]
        pair1 = permute(fence(message1, other)[0], swap)

        def after(value, *events):
            return fence(value, *events)[0]


        one, zero = jnp.ones_like(own), jnp.zeros_like(own)
        both = own * other
        mine_n, mine_f = ways(jnp.where(second, one, other), jnp.where(second, other, one))
        theirs_n, theirs_f = ways(jnp.where(second, own, one), jnp.where(second, one, own))
        seen_n, seen_f = ways(
            jnp.where(second, one, diagonal), jnp.where(second, diagonal, one)
        )
        step_n, step_f = ways(jnp.where(second, both, own), jnp.where(second, own, both))
        pass_n, pass_f = step_n * seen_n, step_f * seen_f
        cross_n, cross_f = ways(jnp.where(second, one, own), jnp.where(second, own, one))
        cross_n = jnp.where(inner, cross_n * seen_n, zero)
        cross_f = cross_f * seen_f
        with_n, with_f = ways(jnp.where(second, zero, one), jnp.where(second, one, zero))
        last_n, last_f = ways(jnp.where(second, other, one), jnp.where(second, one, other))
        mate_n, mate_f = ways(jnp.where(second, one, zero), jnp.where(second, zero, one))
        reach_n = jnp.where(inner, last_n, zero)

        def at(row, k):
            return row[:, k * WIDE : (k + 1) * WIDE]

        mid2 = permute(at(pass_n, 2) * hop2 + near2, middle)
        hop3 = permute(after(near3, hop2), steps)
        gb, gc = local(0, after(rows, hop2), none, none)

        sum0 = at(mine_n, 0) * pairs[0][:STATE] + at(theirs_n, 0) * pair0[:STATE]
        side2 = permute(jnp.where(inner, at(pass_f, 2) * mid2 + far2, sum0), steps)
        mid3 = permute(at(pass_n, 3) * hop3 + near3, middle)
        cross2 = permute(at(cross_n, 2) * hop2 + at(with_n, 2) * near2, swap)
        gb, gc = local(1, after(rows, mid2), gb, gc)

        sum1 = at(mine_n, 1) * message1[:STATE] + at(theirs_n, 1) * pair1[:STATE]
        side3 = permute(jnp.where(inner, at(pass_f, 3) * mid3 + far3, sum1), steps)
        mid0 = permute(at(both, 0) * side2 + sum0, middle)
        end2 = at(cross_f, 2) * jnp.where(inner, mid2, side2) + at(with_f, 2) * far2
        cross2f = permute(end2, swap)
        cross3 = permute(at(cross_n, 3) * hop3 + at(with_n, 3) * near3, swap)
        gb, gc = local(2, after(rows, side2), gb, gc)

        rest0 = at(mine_f, 0) * pairs[0][STATE:] + at(theirs_f, 0) * pair0[STATE:]
        last0 = permute(at(both, 0) * mid0 + rest0, steps)
        mid1 = permute(at(both, 1) * side3 + sum1, middle)
        end3 = at(cross_f, 3) * jnp.where(inner, mid3, side3) + at(with_f, 3) * far3
        cross3f = permute(end3, swap)
        gb, gc = local(3, after(rows, side3), gb, gc)

        rest1 = at(mine_f, 1) * message1[STATE:] + at(theirs_f, 1) * pair1[STATE:]
        last1 = permute(at(both, 1) * mid1 + rest1, steps)

        def entering(k, first, near, middle, far, got_near, got_far):
            far = jnp.where(inner, middle, far)
            if first:
                near = at(reach_n, k) * near + at(mate_n, k) * got_near
                far = at(last_f, k) * far + at(mate_f, k) * got_far
            else:
                near = at(reach_n * seen_n, k) * near + got_near
                far = at(last_f * seen_f, k) * far + got_far
            return ways(near, far)

        enter0 = entering(0, True, side2, mid0, last0, pair0[:STATE], pair0[STATE:])
        *far[0], gb, gc = carried(0, enter0, gb, gc)
        enter2 = entering(2, False, hop2, mid2, side2, cross2, cross2f)
        *far[2], gb, gc = carried(2, enter2, gb, gc)
        cross3f, gb, gc = fence(cross3f, gb, gc)
        enter3 = entering(3, False, hop3, mid3, side3, cross3, cross3f)
        *far[3], gb, gc = carried(3, enter3, gb, gc)
        last1, gb, gc = fence(last1, gb, gc)
        enter1 = entering(1, True, side3, mid1, last1, pair1[:STATE], pair1[STATE:])
        *far[1], gb, gc = carried(1, enter1, gb, gc)
    else:
        gb = gc = none
        for k in range(chunks):
            gb, gc = local(k, rows, gb, gc)
            first = k < late
            lanes = slice(k * WIDE, (k + 1) * WIDE)
            message = pairs[k] if first else jnp.concatenate(sides[k - late], axis=0)
            flipped = jnp.concatenate([message[STATE:], message[:STATE]], axis=0)
            message = jnp.where(lower, message, flipped)
            chunk = Chunk(
                first, message, own[:, lanes], other[:, lanes], diagonal[:, lanes], second
            )
            if first:
                chunk.joined(permute(message, swap))
            group_scan(chunk, group, groups)
            got = None if first else permute(chunk.message(), swap)
            *far[k], gb, gc = carried(k, chunk.entering(got), gb, gc)
    grad_x = jnp.concatenate([item[0] for item in far], axis=1)
    grad_decay = suffix_sums([item[3] for item in near], *([item[i] for item in far] for i in (1, 2, 3)))

    ranks = lax.axis_size("head")
    rank = lax.axis_index("head")
    size = gb.shape[0] // ranks
    sums = jnp.stack([gb, gc])

    def piece(owner):
        return lax.dynamic_slice_in_dim(sums, owner * size, size, axis=1)

    parts = [piece(rank)]
    for step in range(1, ranks):
        links = [(i, i ^ step) for i in range(ranks)]
        parts.append(lax.ppermute(piece(rank ^ step), "head", links))
    grad_b, grad_c = (sum(part[i] for part in parts) for i in range(2))
    return grad_x, grad_b, grad_c, grad_decay


def solution(mesh):
    placed = (P("ctx", "head"), P("ctx", "head"), P("ctx", None), P("ctx", None), P("head", "ctx"))
    return jax.shard_map(
        shards,
        mesh=mesh,
        in_specs=placed,
        out_specs=(
            P("ctx", "head"),
            P(("ctx", "head"), None),
            P(("ctx", "head"), None),
            P("head", "ctx"),
        ),
        check_vma=False,
    )
```

```python
import functools

import jax
import jax.numpy as jnp
from jax import lax
from jax.experimental import pallas as pl
from jax.experimental.pallas import tpu as pltpu
from jax.sharding import PartitionSpec as P

HEAD_DIM = 64
STATE = 128
HEADS = 8
WIDE = HEADS * HEAD_DIM

F32 = jnp.float32
BF16 = jnp.bfloat16
HIGHEST = lax.Precision.HIGHEST
NN = (((1,), (0,)), ((), ()))
NT = (((1,), (1,)), ((), ()))
TN = (((0,), (0,)), ((), ()))
VMEM_LIMIT = 16 * 1024 * 1024
VMEM_ALL = 61 * 1024 * 1024


def dot(a, b, dims=NN):
    return lax.dot_general(a, b, dims, preferred_element_type=F32)


def dot_full(a, b, dims=NN):
    return lax.dot_general(a, b, dims, precision=HIGHEST, preferred_element_type=F32)


def halves(a):
    high = a.astype(BF16)
    return high, (a - high.astype(F32)).astype(BF16)


def dot_halves(a, b, dims=NN):
    high, low = halves(a)
    return dot(high, b, dims) + dot(low, b, dims)


def at_least(shape, row_dim, col_dim):
    return lax.broadcasted_iota(jnp.int32, shape, row_dim) >= lax.broadcasted_iota(
        jnp.int32, shape, col_dim
    )


def spread_matrix(heads):
    shape = (heads, heads * HEAD_DIM)
    lane = lax.broadcasted_iota(jnp.int32, shape, 1)
    first = lax.broadcasted_iota(jnp.int32, shape, 0) * HEAD_DIM
    return jnp.where((lane >= first) & (lane < first + HEAD_DIM), 1.0, 0.0).astype(F32)


def lower_ones(length, row_dim, col_dim):
    return jnp.where(at_least((length, length), row_dim, col_dim), 1.0, 0.0).astype(F32)


def per_head(values):
    spread = spread_matrix(values.shape[1] // HEAD_DIM).astype(BF16)
    high, low = halves(values)
    return dot(spread, high, NT) + dot(spread, low, NT)


def first_half(rows):
    return lax.broadcasted_iota(jnp.int32, (rows, 2 * HEAD_DIM), 1) < HEAD_DIM


def over_lanes(columns):
    rows, heads = columns.shape
    half = first_half(rows)
    parts = []
    for head in range(0, heads, 2):
        left = jnp.broadcast_to(columns[:, head : head + 1], half.shape)
        right = jnp.broadcast_to(columns[:, head + 1 : head + 2], half.shape)
        parts.append(jnp.where(half, left, right))
    return jnp.concatenate(parts, axis=1)


def local_kernel(groups, decay_in, x_in, dy_in, b_in, c_in, *refs):
    chunks = x_in.shape[1] // WIDE
    late = chunks // 2
    count = 5 + chunks + late
    lower = lax.axis_index("ctx") // 2 < groups // 2
    near_at = pl.multiple_of(jnp.where(lower, 0, STATE), STATE)
    far_at = pl.multiple_of(jnp.where(lower, STATE, 0), STATE)
    outs = refs[:count]
    decay_ref, x_ref, dy_ref, b_ref, c_ref = refs[count : count + 5]
    kept = refs[count + 5 : count + 10]
    rows_ref, columns_ref, into_ref, from_ref, totals_ref = kept
    messages, small_sem, wide_sem, out_sem = refs[count + 10 :]
    pending = []

    def leave(source, target):
        copy = pltpu.make_async_copy(source, target, out_sem.at[len(pending)])
        copy.start()
        pending.append(copy)

    small = [
        pltpu.make_async_copy(source, target, small_sem.at[i])
        for i, (source, target) in enumerate(((decay_in, decay_ref), (b_in, b_ref), (c_in, c_ref)))
    ]
    wide = []
    for chunk in range(chunks):
        lanes = pl.ds(chunk * WIDE, WIDE)
        wide.append(
            [
                pltpu.make_async_copy(source.at[:, lanes], target.at[:, lanes], wide_sem.at[i, chunk])
                for i, (source, target) in enumerate(((x_in, x_ref), (dy_in, dy_ref)))
            ]
        )
    for copy in small + [copy for pair in wide for copy in pair]:
        copy.start()
    small[0].wait()
    length = decay_ref.shape[1]
    rows = dot_full(decay_ref[...], lower_ones(length, 1, 0))
    rows_ref[...] = rows
    columns = rows.T
    into_end = jnp.exp(rows[:, length - 1 : length] - rows)
    from_start = jnp.exp(rows)
    into_column = into_end.T
    from_column = from_start.T
    for chunk in range(chunks):
        heads = slice(chunk * HEADS, (chunk + 1) * HEADS)
        columns_ref[chunk] = columns[:, heads]
        into_ref[chunk] = into_column[:, heads]
        from_ref[chunk] = from_column[:, heads]
    for source, target in zip(kept[:4], outs[:4]):
        leave(source, target)
    small[1].wait()
    small[2].wait()
    b_t = b_ref[...].astype(F32).T
    c_t = c_ref[...].astype(F32).T
    half = first_half(STATE)

    def gathered(proj, factors, values_ref, pair):
        head = 2 * pair
        scaled = jnp.concatenate(
            [proj * factors[head : head + 1, :], proj * factors[head + 1 : head + 2, :]], axis=0
        )
        sums = dot(scaled.astype(BF16), values_ref[:, pl.ds(pair * STATE, STATE)])
        return jnp.where(half, sums[:STATE], sums[STATE:])

    for chunk in range(chunks):
        lanes = pl.ds(chunk * WIDE, WIDE)
        heads = slice(chunk * HEADS, (chunk + 1) * HEADS)
        pairs = range(chunk * HEADS // 2, (chunk + 1) * HEADS // 2)
        totals_ref[:, lanes] = over_lanes(from_column[length - 8 :, heads])[7:8, :]
        for place, (proj, factors, values_ref, rows_at) in enumerate(
            ((b_t, into_end, x_ref, near_at), (c_t, from_start, dy_ref, far_at))
        ):
            wide[chunk][place].wait()
            for pair in pairs:
                at = (pair - pairs[0]) * STATE
                messages[chunk, pl.ds(rows_at, STATE), at : at + STATE] = gathered(
                    proj, factors, values_ref, pair
                )
        if chunk < chunks - late:
            leave(messages.at[chunk], outs[5 + chunk])
        else:
            place = 5 + late + 2 * (chunk - late)
            leave(messages.at[chunk, :STATE], outs[place])
            leave(messages.at[chunk, STATE:], outs[place + 1])
    leave(totals_ref, outs[4])
    for copy in pending:
        copy.wait()


def intra_kernel(
    rows_ref,
    columns_ref,
    into_ref,
    from_ref,
    x_ref,
    dy_ref,
    b_ref,
    c_ref,
    gb_in_ref,
    gc_in_ref,
    dx_ref,
    xs_ref,
    dys_ref,
    change_ref,
    gb_ref,
    gc_ref,
    table_ref,
):
    step = pl.program_id(0)
    rows = rows_ref[...]
    columns = columns_ref[0]
    xs_ref[...] = (x_ref[...].astype(F32) * over_lanes(into_ref[0])).astype(BF16)
    dys_ref[...] = (dy_ref[...].astype(F32) * over_lanes(from_ref[0])).astype(BF16)
    length = rows.shape[1]
    b, c = b_ref[...], c_ref[...]
    scores = dot(b, c, NT)
    size = STATE
    keep = at_least((size, size), 1, 0)
    half = first_half(size)
    blocks = length // size

    @pl.when(step == 0)
    def _():
        table_ref[...] = jnp.zeros_like(table_ref)


    for pair in range(HEADS // 2):
        lanes = slice(pair * 2 * HEAD_DIM, (pair + 1) * 2 * HEAD_DIM)
        dy2 = dy_ref[:, lanes]
        sums = [None, None]
        for block in range(blocks):
            first = block * size
            x2 = x_ref[first : first + size, lanes].astype(F32)
            parts = []
            for side in range(2):
                head = 2 * pair + side
                own = half if side == 0 else jnp.logical_not(half)
                x1 = jnp.where(own, x2, 0.0).astype(BF16)
                pairs = dot(x1, dy2[first:], NT)
                gap = rows[head : head + 1, first:] - columns[first : first + size, head : head + 1]
                near = jnp.where(keep, gap[:, :size], -1e30)
                if length - first > size:
                    near = jnp.concatenate([near, gap[:, size:]], axis=1)
                mask = jnp.exp(near)
                weights = (mask * scores[first : first + size, first:]).astype(BF16)
                table_ref[first : first + size, first:] += mask * pairs
                change = jnp.sum(weights.astype(F32) * pairs, axis=0, keepdims=True)
                if block == 0:
                    sums[side] = change
                else:
                    sums[side] = jnp.concatenate(
                        [sums[side][:, :first], sums[side][:, first:] + change], axis=1
                    )
                parts.append(dot(weights, dy2[first:]))
            dx_ref[first : first + size, lanes] = jnp.where(half, parts[0], parts[1])
        for side in range(2):
            head = 2 * pair + side
            change_ref[head : head + 1, :] = sums[side]

    change_ref[...] -= per_head(x_ref[...].astype(F32) * dx_ref[...])

    @pl.when(step == pl.num_programs(0) - 1)
    def _():
        table = table_ref[...]
        gb_ref[...] = gb_in_ref[...] + dot_halves(table, c)
        gc_ref[...] = gc_in_ref[...] + dot_halves(table, b, TN)


def inter_kernel(
    chunk,
    into_ref,
    state_in_ref,
    adjoint_in_ref,
    total_ref,
    xs_ref,
    dys_ref,
    b_ref,
    c_ref,
    dx_ref,
    gb_ref,
    gc_ref,
    gx_ref,
    change_ref,
    earlier_ref,
    later_ref,
    gb_out_ref,
    gc_out_ref,
):
    lanes = slice(chunk * WIDE, (chunk + 1) * WIDE)
    state_in = state_in_ref[...]
    adjoint_in = adjoint_in_ref[...]
    state_low = state_in.astype(BF16)
    adjoint_low = adjoint_in.astype(BF16)
    xs = xs_ref[...]
    dys = dys_ref[...]
    gb_out_ref[...] = gb_ref[...] + dot(xs, adjoint_low, NT)
    gc_out_ref[...] = gc_ref[...] + dot(dys, state_low, NT)
    outer = dot(b_ref[...], adjoint_low)
    gx_ref[...] = (dx_ref[...] + over_lanes(into_ref[chunk]) * outer).astype(BF16)
    spread = spread_matrix(HEADS).astype(BF16)
    change = dys.astype(F32) * dot(c_ref[...], state_low)
    change_ref[...] = dot(spread, change.astype(BF16), NT)
    earlier_ref[...] = dot(spread, (xs.astype(F32) * outer).astype(BF16), NT)
    later_ref[...] = per_head(total_ref[:, lanes] * state_in * adjoint_in)


def suffix_kernel(chunks, *refs):
    out_ref = refs[-1]
    length = out_ref.shape[1]

    def joined(place):
        return jnp.concatenate([ref[...] for ref in refs[place * chunks : (place + 1) * chunks]], 0)

    from_here = dot_full(joined(0) + joined(1), lower_ones(length, 0, 1))
    before = dot_full(joined(2), 1.0 - lower_ones(length, 0, 1))
    out_ref[...] = from_here + before + jnp.sum(joined(3), axis=1, keepdims=True)


def params(limit=VMEM_LIMIT):
    return pltpu.CompilerParams(vmem_limit_bytes=limit)


def cost(flops, nbytes):
    return pl.CostEstimate(flops=flops, bytes_accessed=nbytes, transcendentals=0)


def shape(dims, dtype=F32):
    return jax.ShapeDtypeStruct(dims, dtype)


def vmem(count):
    return [pl.BlockSpec(memory_space=pltpu.VMEM)] * count


def local_states(groups, log_decay, x, dy, b, c):
    tokens, width = x.shape
    heads = log_decay.shape[0]
    chunks = width // WIDE
    kept = [(heads, tokens)] + [(chunks, tokens, HEADS)] * 3 + [(1, width)]
    late = chunks // 2
    outs = kept + [(2 * STATE, WIDE)] * (chunks - late) + [(STATE, WIDE)] * (2 * late)
    hbm = pl.BlockSpec(memory_space=pltpu.HBM)
    outs = pl.pallas_call(
        functools.partial(local_kernel, groups),
        in_specs=[hbm] * 5,
        out_specs=[hbm] * len(outs),
        out_shape=[shape(dims) for dims in outs],
        scratch_shapes=[
            pltpu.VMEM(log_decay.shape, F32),
            pltpu.VMEM(x.shape, BF16),
            pltpu.VMEM(x.shape, BF16),
            pltpu.VMEM(b.shape, BF16),
            pltpu.VMEM(b.shape, BF16),
            *[pltpu.VMEM(dims, F32) for dims in kept],
            pltpu.VMEM((chunks, 2 * STATE, WIDE), F32),
            pltpu.SemaphoreType.DMA((3,)),
            pltpu.SemaphoreType.DMA((2, chunks)),
            pltpu.SemaphoreType.DMA((len(outs),)),
        ],
        compiler_params=params(VMEM_ALL),
        cost_estimate=cost(4 * tokens * STATE * width, 12 * tokens * width),
        name="local_states",
    )(log_decay, x, dy, b, c)
    pairs, sides = outs[5 : 5 + chunks - late], outs[5 + chunks - late :]
    return outs[:5], pairs, [sides[i : i + 2] for i in range(0, 2 * late, 2)]


def intra(chunk, rows, columns, into, start, x, dy, b, c, gb, gc):
    tokens = x.shape[0]
    wide = pl.BlockSpec((tokens, WIDE), lambda k: (0, chunk))
    own = pl.BlockSpec((tokens, WIDE), lambda k: (0, 0))
    proj = pl.BlockSpec((tokens, STATE), lambda k: (0, 0))
    return pl.pallas_call(
        intra_kernel,
        grid=(1,),
        in_specs=[
            pl.BlockSpec((HEADS, tokens), lambda k: (chunk, 0)),
            *[pl.BlockSpec((1, tokens, HEADS), lambda k: (chunk, 0, 0))] * 3,
            wide,
            wide,
            *[proj] * 4,
        ],
        out_specs=[own, own, own, pl.BlockSpec((HEADS, tokens), lambda k: (0, 0)), proj, proj],
        out_shape=[
            shape((tokens, WIDE)),
            shape((tokens, WIDE), BF16),
            shape((tokens, WIDE), BF16),
            shape((HEADS, tokens)),
            shape((tokens, STATE)),
            shape((tokens, STATE)),
        ],
        scratch_shapes=[pltpu.VMEM((tokens, tokens), F32)],
        compiler_params=params(),
        cost_estimate=cost(4 * tokens * tokens * WIDE, 8 * tokens * WIDE),
        name="intra",
    )(rows, columns, into, start, x, dy, b, c, gb, gc)


def inter(chunk, into, state_in, adjoint_in, totals, xs, dys, b, c, dx, gb, gc):
    tokens = xs.shape[0]
    args = (into, state_in, adjoint_in, totals, xs, dys, b, c, dx, gb, gc)
    out_shape = [
        shape((tokens, WIDE), BF16),
        shape((HEADS, tokens)),
        shape((HEADS, tokens)),
        shape((HEADS, STATE)),
        shape((tokens, STATE)),
        shape((tokens, STATE)),
    ]
    return pl.pallas_call(
        functools.partial(inter_kernel, chunk),
        in_specs=vmem(len(args)),
        out_specs=vmem(len(out_shape)),
        out_shape=out_shape,
        compiler_params=params(),
        cost_estimate=cost(8 * tokens * STATE * WIDE, 16 * tokens * WIDE),
        name="inter",
    )(*args)


def suffix_sums(*parts):
    chunks = len(parts[0])
    args = [item for part in parts for item in part]
    return pl.pallas_call(
        functools.partial(suffix_kernel, chunks),
        in_specs=vmem(len(args)),
        out_specs=vmem(1)[0],
        out_shape=shape((chunks * HEADS, args[0].shape[1])),
        compiler_params=params(),
        cost_estimate=cost(0, 1 << 17),
        name="suffix_sums",
    )(*args)


class Chunk:
    def __init__(self, first, message, own, other, diagonal, second):
        self.first, self.own, self.other, self.second = first, own, other, second
        self.state, self.adjoint = message[:STATE], message[STATE:]
        both = own * other
        if first:
            self.step_f = self.step_b = both
            self.seen_f = self.seen_b = jnp.ones_like(own)
        else:
            self.forward, self.backward = self.state, self.adjoint
            self.step_f, self.step_b = jnp.where(second, both, own), jnp.where(second, own, both)
            self.seen_f = jnp.where(second, 1.0, diagonal)
            self.seen_b = jnp.where(second, diagonal, 1.0)

    def joined(self, got):
        self.got_f, self.got_b = got[:STATE], got[STATE:]
        own, other = self.own, self.other
        self.forward = jnp.where(
            self.second, own * self.got_f + self.state, other * self.state + self.got_f
        )
        self.backward = jnp.where(
            self.second, self.got_b + other * self.adjoint, self.adjoint + own * self.got_b
        )

    def leaving_f(self, carried):
        return self.step_f * carried + self.forward

    def leaving_b(self, carried):
        return self.step_b * carried + self.backward

    def message(self):
        send_f = jnp.where(self.second, self.in_f, self.own * self.in_f + self.state)
        send_b = jnp.where(self.second, self.own * self.in_b + self.adjoint, self.in_b)
        return jnp.concatenate([send_f, send_b], axis=0)

    def entering(self, got=None):
        decayed_f = jnp.where(self.second, self.other, 1.0) * self.in_f
        decayed_b = jnp.where(self.second, 1.0, self.other) * self.in_b
        if got is not None:
            return decayed_f + got[:STATE], decayed_b + got[STATE:]
        return (
            decayed_f + jnp.where(self.second, self.got_f, 0.0),
            decayed_b + jnp.where(self.second, 0.0, self.got_b),
        )


def between(links):
    return [(2 * s + side, 2 * t + side) for s, t in links for side in range(2)]


def group_scan(chunk, group, groups):
    carried_f, carried_b = jnp.zeros_like(chunk.forward), jnp.zeros_like(chunk.backward)
    for hop in range(1, groups):
        send = jnp.where(
            group == groups - hop, chunk.leaving_b(carried_b), chunk.leaving_f(carried_f)
        )
        links = [(hop - 1, hop), (groups - hop, groups - hop - 1)]
        got = lax.ppermute(send, "ctx", between(links))
        carried_f = jnp.where(group == hop, chunk.seen_f * got, carried_f)
        carried_b = jnp.where(group == groups - hop - 1, chunk.seen_b * got, carried_b)
    chunk.in_f, chunk.in_b = carried_f, carried_b


def fence(*items):
    return lax.optimization_barrier(items)


def shards(inputs, grad_out, b_proj, c_proj, log_decay):
    count = lax.axis_size("ctx")
    mine = lax.axis_index("ctx")
    second = mine % 2 == 1
    group, groups = mine // 2, count // 2

    def permute(value, links):
        return lax.ppermute(value, "ctx", links)

    swap = [(i, i ^ 1) for i in range(count)]
    diagonals = [(2 * g + 1, 2 * g + 2) for g in range(groups - 1)]
    diagonals += [(t, s) for s, t in diagonals]
    lower = group < groups // 2
    inner = (group > 0) & (group < groups - 1)

    (rows, columns, into, start, totals), pairs, sides = local_states(
        groups, log_decay, inputs, grad_out, b_proj, c_proj
    )
    late = len(pairs)
    chunks = late + len(sides)
    own = totals
    other = permute(own, swap)
    diagonal = permute(own, diagonals)
    none = jnp.zeros((inputs.shape[0], STATE), F32)
    near = [None] * chunks

    def local(k, rows, gb, gc):
        *near[k], gb, gc = intra(
            k, rows, columns, into, start, inputs, grad_out, b_proj, c_proj, gb, gc
        )
        return gb, gc

    def carried(k, entering, gb, gc):
        dx, xs, dys, _ = near[k]
        return inter(k, into, *entering, totals, xs, dys, b_proj, c_proj, dx, gb, gc)

    def ways(forward, backward):
        return jnp.where(lower, forward, backward), jnp.where(lower, backward, forward)

    far = [None] * chunks
    if groups == 4 and chunks == 4:
        middle = between([(1, 2), (2, 1)])
        steps = between([(0, 1), (1, 0), (2, 3), (3, 2)])
        (near2, far2), (near3, far3) = sides

        pair0 = permute(pairs[0], swap)
        hop2 = permute(near2, steps)
        message1 = pairs[1]
        pair1 = permute(fence(message1, other)[0], swap)

        def after(value, *events):
            return fence(value, *events)[0]


        one, zero = jnp.ones_like(own), jnp.zeros_like(own)
        both = own * other
        mine_n, mine_f = ways(jnp.where(second, one, other), jnp.where(second, other, one))
        theirs_n, theirs_f = ways(jnp.where(second, own, one), jnp.where(second, one, own))
        seen_n, seen_f = ways(
            jnp.where(second, one, diagonal), jnp.where(second, diagonal, one)
        )
        step_n, step_f = ways(jnp.where(second, both, own), jnp.where(second, own, both))
        pass_n, pass_f = step_n * seen_n, step_f * seen_f
        cross_n, cross_f = ways(jnp.where(second, one, own), jnp.where(second, own, one))
        cross_n = jnp.where(inner, cross_n * seen_n, zero)
        cross_f = cross_f * seen_f
        with_n, with_f = ways(jnp.where(second, zero, one), jnp.where(second, one, zero))
        last_n, last_f = ways(jnp.where(second, other, one), jnp.where(second, one, other))
        mate_n, mate_f = ways(jnp.where(second, one, zero), jnp.where(second, zero, one))
        reach_n = jnp.where(inner, last_n, zero)

        def at(row, k):
            return row[:, k * WIDE : (k + 1) * WIDE]

        mid2 = permute(at(pass_n, 2) * hop2 + near2, middle)
        hop3 = permute(after(near3, hop2), steps)
        gb, gc = local(0, after(rows, hop2), none, none)

        sum0 = at(mine_n, 0) * pairs[0][:STATE] + at(theirs_n, 0) * pair0[:STATE]
        side2 = permute(jnp.where(inner, at(pass_f, 2) * mid2 + far2, sum0), steps)
        mid3 = permute(at(pass_n, 3) * hop3 + near3, middle)
        cross2 = permute(at(cross_n, 2) * hop2 + at(with_n, 2) * near2, swap)
        gb, gc = local(1, after(rows, mid2), gb, gc)

        sum1 = at(mine_n, 1) * message1[:STATE] + at(theirs_n, 1) * pair1[:STATE]
        side3 = permute(jnp.where(inner, at(pass_f, 3) * mid3 + far3, sum1), steps)
        mid0 = permute(at(both, 0) * side2 + sum0, middle)
        end2 = at(cross_f, 2) * jnp.where(inner, mid2, side2) + at(with_f, 2) * far2
        cross2f = permute(end2, swap)
        cross3 = permute(at(cross_n, 3) * hop3 + at(with_n, 3) * near3, swap)
        gb, gc = local(2, after(rows, side2), gb, gc)

        rest0 = at(mine_f, 0) * pairs[0][STATE:] + at(theirs_f, 0) * pair0[STATE:]
        last0 = permute(at(both, 0) * mid0 + rest0, steps)
        mid1 = permute(at(both, 1) * side3 + sum1, middle)
        end3 = at(cross_f, 3) * jnp.where(inner, mid3, side3) + at(with_f, 3) * far3
        cross3f = permute(end3, swap)
        gb, gc = local(3, after(rows, side3), gb, gc)

        rest1 = at(mine_f, 1) * message1[STATE:] + at(theirs_f, 1) * pair1[STATE:]
        last1 = permute(at(both, 1) * mid1 + rest1, steps)

        def entering(k, first, near, middle, far, got_near, got_far):
            far = jnp.where(inner, middle, far)
            if first:
                near = at(reach_n, k) * near + at(mate_n, k) * got_near
                far = at(last_f, k) * far + at(mate_f, k) * got_far
            else:
                near = at(reach_n * seen_n, k) * near + got_near
                far = at(last_f * seen_f, k) * far + got_far
            return ways(near, far)

        enter0 = entering(0, True, side2, mid0, last0, pair0[:STATE], pair0[STATE:])
        *far[0], gb, gc = carried(0, enter0, gb, gc)
        enter2 = entering(2, False, hop2, mid2, side2, cross2, cross2f)
        *far[2], gb, gc = carried(2, enter2, gb, gc)
        cross3f, gb, gc = fence(cross3f, gb, gc)
        enter3 = entering(3, False, hop3, mid3, side3, cross3, cross3f)
        *far[3], gb, gc = carried(3, enter3, gb, gc)
        last1, gb, gc = fence(last1, gb, gc)
        enter1 = entering(1, True, side3, mid1, last1, pair1[:STATE], pair1[STATE:])
        *far[1], gb, gc = carried(1, enter1, gb, gc)
    else:
        gb = gc = none
        for k in range(chunks):
            gb, gc = local(k, rows, gb, gc)
            first = k < late
            lanes = slice(k * WIDE, (k + 1) * WIDE)
            message = pairs[k] if first else jnp.concatenate(sides[k - late], axis=0)
            flipped = jnp.concatenate([message[STATE:], message[:STATE]], axis=0)
            message = jnp.where(lower, message, flipped)
            chunk = Chunk(
                first, message, own[:, lanes], other[:, lanes], diagonal[:, lanes], second
            )
            if first:
                chunk.joined(permute(message, swap))
            group_scan(chunk, group, groups)
            got = None if first else permute(chunk.message(), swap)
            *far[k], gb, gc = carried(k, chunk.entering(got), gb, gc)
    grad_x = jnp.concatenate([item[0] for item in far], axis=1)
    grad_decay = suffix_sums([item[3] for item in near], *([item[i] for item in far] for i in (1, 2, 3)))

    ranks = lax.axis_size("head")
    rank = lax.axis_index("head")
    size = gb.shape[0] // ranks
    sums = jnp.stack([gb, gc])

    def piece(owner):
        return lax.dynamic_slice_in_dim(sums, owner * size, size, axis=1)

    parts = [piece(rank)]
    for step in range(1, ranks):
        links = [(i, i ^ step) for i in range(ranks)]
        parts.append(lax.ppermute(piece(rank ^ step), "head", links))
    grad_b, grad_c = (sum(part[i] for part in parts) for i in range(2))
    return grad_x, grad_b, grad_c, grad_decay


def solution(mesh):
    placed = (P("ctx", "head"), P("ctx", "head"), P("ctx", None), P("ctx", None), P("head", "ctx"))
    return jax.shard_map(
        shards,
        mesh=mesh,
        in_specs=placed,
        out_specs=(
            P("ctx", "head"),
            P(("ctx", "head"), None),
            P(("ctx", "head"), None),
            P("head", "ctx"),
        ),
        check_vma=False,
    )
```
